256 devices in a mesh: gx: 128 (over z, x, y), ta: 2 (over core).
Axes of the slice: x: 4, y: 4, z: 8, core: 2. Of those that a mesh axis runs over, the one named last changes fastest.
Arguments:
- embeddings: bfloat16 [131072, 512], P('gx'), may hold values from -12 to 12
- labels: bfloat16 [131072, 256], P('gx'), may hold values from -6 to 6
- bucket_ids: int32 [2, 131072, 1], P('ta', 'gx'), may hold values from 0 to 127, as said below
Outputs:
- diffused: float32 [131072, 256], P('gx')
The draws below stay inside these ranges and needn't reach their ends.
Inputs may be any that keep to these rules, and one draw needn't show every extreme that they name: `bucket_ids`: in each table, the items of one index of gx name any one bucket at most 16 times; in each table one bucket is named exactly 16 times by the items of every index of gx.
All inputs are finite; a program needn't handle non-finite values.
Results may differ from the reference program's by a relative error of at most 0.00032.
Values may be sent and summed in bfloat16 or wider, within the bound.
A program may use at most 64 MiB of HBM per device.

```python
import jax
import jax.numpy as jnp
from jax import lax

E = 512
L = 256
CAP = 2048
ROWS_DEV = 1024
TABLES = 2
ROWS = 131072
NBUCK = 128
SLOT = 16
N_GX = 128


def bucket_table(key):
    base_key = jax.random.fold_in(key, 11)
    table_keys = jax.random.split(jax.random.fold_in(base_key, 1), TABLES)
    bucket_rank = jax.vmap(lambda one_key: jax.random.permutation(one_key, NBUCK))(table_keys)
    popularity = jnp.where(bucket_rank == 0, 16384, jnp.where(bucket_rank <= NBUCK // 4, 4096, 0)).astype(jnp.int32)
    blocks_count = ROWS // ROWS_DEV
    slot_index = jnp.arange(CAP, dtype=jnp.int32).reshape(NBUCK, SLOT)

    def one_block(block_key, table_boost):
        jitter_key, shuffle_key = jax.random.split(block_key)
        jitter = jax.random.randint(jitter_key, (NBUCK, SLOT), 0, 8192, dtype=jnp.int32)
        ranking = (jitter + table_boost[:, None]) * CAP + slot_index
        chosen = lax.top_k(ranking.reshape(-1), ROWS_DEV)[1]
        bucket = (chosen // SLOT).astype(jnp.int32)
        shuffle = jax.random.permutation(shuffle_key, ROWS_DEV)
        return bucket[shuffle]
    flat_keys = jax.random.split(jax.random.fold_in(base_key, 2), TABLES * blocks_count)
    flat_boost = jnp.repeat(popularity, blocks_count, axis=0)
    bucket_rows = jax.vmap(one_block)(flat_keys, flat_boost)
    return bucket_rows.reshape(TABLES, ROWS, 1).astype(jnp.int32)


def draw_bucket_ids(key, part):
    return bucket_table(key)


def draw_embeddings(key, part):
    bucket_rows = bucket_table(key)[:, :, 0]
    float_key = jax.random.fold_in(key, 12)
    center_key, weight_key, jitter_key = jax.random.split(float_key, 3)
    centers = jax.random.normal(center_key, (TABLES, NBUCK, E), jnp.float32)
    weights = jax.random.uniform(weight_key, (TABLES, ROWS), jnp.float32, 0.3, 2.0)
    jitter = 0.5 * jax.random.normal(jitter_key, (ROWS, E), jnp.float32)
    total = jitter
    for table in range(TABLES):
        total = total + weights[table][:, None] * centers[table][bucket_rows[table]]
    return jnp.clip(total, -12.0, 12.0).astype(jnp.bfloat16)


def levels(stream_key, dims, cuts, low, top_value):
    loudness, own = 1.0, jax.random.fold_in(stream_key, 6)
    for position, blocks in cuts:
        heights = jnp.exp(jax.random.uniform(jax.random.fold_in(own, position), (blocks,), jnp.float32, low / len(cuts), top_value / len(cuts)))
        loudness = loudness * jnp.repeat(heights, dims[position] // blocks).reshape([-1 if axis == position else 1 for axis in range(len(dims))])
    return loudness


def normal_values(rng, extent, spread, bound, shards=(), kind=jnp.bfloat16):
    values = spread * jax.random.normal(rng, extent, jnp.float32)
    if shards:
        values = values * levels(rng, extent, shards, -0.22, 0.18)
    return jnp.clip(values, -bound, bound).astype(kind)


def setup_inputs(seed: int = 0) -> dict:
    streams_of = jax.random.split(jax.random.key(seed), 4)
    return {
        "embeddings": draw_embeddings(jax.random.fold_in(streams_of[3], 71), 0),
        "labels": normal_values(streams_of[1], (ROWS, L), 1.0, 6.0, ((0, 128),)),
        "bucket_ids": draw_bucket_ids(jax.random.fold_in(streams_of[3], 71), 0),
    }


sharpness = 8.0
alpha_mix = 0.8

def normalize(embeds):
    wide = embeds.astype(jnp.float32)
    return (wide * lax.rsqrt(lax.optimization_barrier(jnp.sum(wide * wide, axis=1, keepdims=True)) + 1e-06)).astype(jnp.bfloat16)

def bucket_sums(unit, feats, valid):
    cap = unit.shape[0]
    block = min(512, cap)
    cols = jnp.arange(cap)
    nums = []
    dens = []
    for start in range(0, cap, block):
        gram = lax.dot_general(unit[start:start + block], unit, (((1,), (1,)), ((), ())), preferred_element_type=jnp.float32)
        keep = valid[None, :] * (cols[None, :] != (start + jnp.arange(block))[:, None]).astype(jnp.float32)
        weights = (jnp.exp(sharpness * gram) * keep).astype(jnp.bfloat16)
        nums.append(jnp.dot(weights, feats, preferred_element_type=jnp.float32))
        dens.append(lax.optimization_barrier(jnp.sum(weights.astype(jnp.float32), axis=1)))
    return (jnp.concatenate(nums, axis=0), jnp.concatenate(dens, axis=0))

def inverse_of(ids):
    per_dev = ids.reshape(N_GX, ROWS_DEV)
    onehot = (per_dev[:, :, None] == jnp.arange(NBUCK, dtype=jnp.int32)[None, None, :]).astype(jnp.int32)
    running = jnp.cumsum(onehot, axis=1)
    rank = lax.optimization_barrier(jnp.sum(running * onehot, axis=2)) - 1
    source = jnp.arange(N_GX, dtype=jnp.int32)[:, None]
    where = (per_dev * CAP + source * SLOT + rank).reshape(-1).astype(jnp.int32)
    inverse = jnp.full((NBUCK * CAP,), ROWS, jnp.int32).at[where].set(jnp.arange(ROWS, dtype=jnp.int32))
    return inverse.reshape(NBUCK, CAP)

def reference(embeddings, labels, bucket_ids):
    unit = normalize(embeddings)
    unit_pad = jnp.concatenate([unit, jnp.zeros((1, E), jnp.bfloat16)], axis=0)
    prior = labels.astype(jnp.float32)
    inverses = [inverse_of(bucket_ids[t, :, 0]) for t in range(bucket_ids.shape[0])]

    def one_round(feats):
        feats_pad = jnp.concatenate([feats, jnp.zeros((1, L), jnp.bfloat16)], axis=0)
        total_num = jnp.zeros((ROWS + 1, L), jnp.float32)
        total_den = jnp.zeros((ROWS + 1,), jnp.float32)
        for inverse in inverses:

            def visit(carry, members):
                acc_num, acc_den = carry
                valid = (members < ROWS).astype(jnp.float32)
                part_num, part_den = bucket_sums(unit_pad[members], feats_pad[members], valid)
                return ((acc_num.at[members].add(part_num), acc_den.at[members].add(part_den)), None)
            start = (jnp.zeros((ROWS + 1, L), jnp.float32), jnp.zeros((ROWS + 1,), jnp.float32))
            (table_num, table_den), unused = lax.scan(visit, start, inverse)
            total_num = total_num + table_num
            total_den = total_den + table_den
        return (1.0 - alpha_mix) * prior + alpha_mix * total_num[:ROWS] / (1.0 + total_den[:ROWS])[:, None]
    first = one_round(labels)
    return one_round(first.astype(jnp.bfloat16))
```

```python
import jax
import jax.numpy as jnp
from jax import lax
from jax.sharding import PartitionSpec as P

CAP = 2048
PAD_MARK = -1024.0


sharpness = 8.0
alpha_mix = 0.8


def normalize(embeds):
    wide = embeds.astype(jnp.float32)
    return (wide * lax.rsqrt(jnp.sum(wide * wide, axis=1, keepdims=True) + 1e-06)).astype(
        jnp.bfloat16
    )


def bucket_weights(unit, valid):
    cap = unit.shape[0]
    block = min(512, cap)
    cols = jnp.arange(cap)
    blocks = []
    dens = []
    for start in range(0, cap, block):
        gram = lax.dot_general(
            unit[start : start + block],
            unit,
            (((1,), (1,)), ((), ())),
            preferred_element_type=jnp.float32,
        )
        keep = valid[None, :] * (cols[None, :] != (start + jnp.arange(block))[:, None]).astype(
            jnp.float32
        )
        weights = (jnp.exp(sharpness * gram) * keep).astype(jnp.bfloat16)
        blocks.append(weights)
        dens.append(jnp.sum(weights.astype(jnp.float32), axis=1))
    return blocks, jnp.concatenate(dens, axis=0)


def weighted_sums(blocks, feats):
    return jnp.concatenate(
        [jnp.dot(w, feats, preferred_element_type=jnp.float32) for w in blocks], axis=0
    )


def body(embeddings, labels, bucket_ids):
    groups = lax.axis_size("gx")
    rows = embeddings.shape[0]
    slot = CAP // groups
    width_l = labels.shape[1]
    ids = bucket_ids[0, :, 0]
    pos = jnp.arange(rows, dtype=jnp.int32)
    same = (ids[:, None] == ids[None, :]) & (pos[None, :] < pos[:, None])
    rank = jnp.sum(same.astype(jnp.int32), axis=1)
    target = ids * slot + rank
    slots = jnp.arange(groups * slot, dtype=jnp.int32)
    place_mat = (target[None, :] == slots[:, None]).astype(jnp.bfloat16)
    occupied = jnp.sum(place_mat.astype(jnp.float32), axis=1) > 0.5
    prior = labels.astype(jnp.float32)

    def place(payload):
        return jnp.dot(place_mat, payload, preferred_element_type=jnp.float32).astype(payload.dtype)

    def exchange(buffer):
        return lax.all_to_all(buffer, "gx", split_axis=0, concat_axis=0, tiled=True)

    def other_core(values):
        return lax.ppermute(values, "ta", perm=[(0, 1), (1, 0)])

    unit_here = normalize(embeddings)
    placed = place(jnp.concatenate([unit_here, labels], axis=1))
    mark = jnp.where(occupied, placed[:, unit_here.shape[1]], PAD_MARK)
    placed = placed.at[:, unit_here.shape[1]].set(mark.astype(jnp.bfloat16))
    got = exchange(placed.reshape(groups, slot, -1)).reshape(groups * slot, -1)
    unit = got[:, : unit_here.shape[1]]
    feats0 = got[:, unit_here.shape[1] :]
    valid = (feats0[:, 0].astype(jnp.float32) > PAD_MARK * 0.5).astype(jnp.float32)

    blocks, den = bucket_weights(unit, valid)
    num1 = weighted_sums(blocks, feats0)

    packed = jnp.concatenate(
        [
            num1.reshape(groups, slot * width_l),
            jnp.pad(den.reshape(groups, slot), ((0, 0), (0, 128 - slot))),
        ],
        axis=1,
    )
    back = exchange(packed)
    back_num = back[:, : slot * width_l].reshape(groups * slot, width_l)
    back_den = back[:, slot * width_l : slot * width_l + slot].reshape(groups * slot)
    row_num = back_num[target]
    row_den = back_den[target]
    other_num, other_den = other_core((row_num, row_den))
    total_num = row_num + other_num
    total_den = row_den + other_den
    scale = (1.0 + total_den)[:, None]
    first = (1.0 - alpha_mix) * prior + alpha_mix * total_num / scale

    feats1 = exchange(place(first.astype(jnp.bfloat16)).reshape(groups, slot, -1))
    num2 = weighted_sums(blocks, feats1.reshape(groups * slot, -1))
    back2 = exchange(num2.reshape(groups, slot, -1)).reshape(groups * slot, -1)
    row_num2 = back2[target]
    total_num2 = row_num2 + other_core(row_num2)
    return (1.0 - alpha_mix) * prior + alpha_mix * total_num2 / scale


def solution(mesh):
    return jax.shard_map(
        body,
        mesh=mesh,
        in_specs=(P("gx", None), P("gx", None), P("ta", "gx", None)),
        out_specs=P("gx", None),
        check_vma=False,
    )
```

```python
import jax
import jax.numpy as jnp
from jax import lax
from jax.sharding import PartitionSpec as P

CAP = 2048
PAD_MARK = -1024.0


sharpness = 8.0
alpha_mix = 0.8


def normalize(embeds):
    wide = embeds.astype(jnp.float32)
    return (wide * lax.rsqrt(jnp.sum(wide * wide, axis=1, keepdims=True) + 1e-06)).astype(
        jnp.bfloat16
    )


def bucket_weights(unit, valid):
    cap = unit.shape[0]
    block = min(512, cap)
    cols = jnp.arange(cap)
    blocks = []
    dens = []
    for start in range(0, cap, block):
        gram = lax.dot_general(
            unit[start : start + block],
            unit,
            (((1,), (1,)), ((), ())),
            preferred_element_type=jnp.float32,
        )
        keep = valid[None, :] * (cols[None, :] != (start + jnp.arange(block))[:, None]).astype(
            jnp.float32
        )
        weights = (jnp.exp(sharpness * gram) * keep).astype(jnp.bfloat16)
        blocks.append(weights)
        dens.append(jnp.sum(weights.astype(jnp.float32), axis=1))
    return blocks, jnp.concatenate(dens, axis=0)


def weighted_sums(blocks, feats):
    return jnp.concatenate(
        [jnp.dot(w, feats, preferred_element_type=jnp.float32) for w in blocks], axis=0
    )


def body(embeddings, labels, bucket_ids, chunks=2):
    groups = lax.axis_size("gx")
    rows = embeddings.shape[0]
    slot = CAP // groups
    width_l = labels.shape[1]
    ids = bucket_ids[0, :, 0]
    pos = jnp.arange(rows, dtype=jnp.int32)
    same = (ids[:, None] == ids[None, :]) & (pos[None, :] < pos[:, None])
    rank = jnp.sum(same.astype(jnp.int32), axis=1)
    target = ids * slot + rank
    slots = jnp.arange(groups * slot, dtype=jnp.int32)
    place_mat = (target[None, :] == slots[:, None]).astype(jnp.bfloat16)
    occupied = jnp.sum(place_mat.astype(jnp.float32), axis=1) > 0.5
    prior = labels.astype(jnp.float32)

    def place(payload):
        return jnp.dot(place_mat, payload, preferred_element_type=jnp.float32).astype(payload.dtype)

    def exchange(buffer):
        return lax.all_to_all(buffer, "gx", split_axis=0, concat_axis=0, tiled=True)

    def other_core(values):
        return lax.ppermute(values, "ta", perm=[(0, 1), (1, 0)])

    unit_here = normalize(embeddings)
    unit = exchange(place(unit_here).reshape(groups, slot, -1)).reshape(groups * slot, -1)
    placed_l = place(labels)
    column = lax.broadcasted_iota(jnp.int32, placed_l.shape, 1)
    placed_l = jnp.where((column == 0) & ~occupied[:, None], jnp.bfloat16(PAD_MARK), placed_l)
    feats0 = exchange(placed_l.reshape(groups, slot, -1)).reshape(groups * slot, -1)
    valid = (feats0[:, 0].astype(jnp.float32) > PAD_MARK * 0.5).astype(jnp.float32)

    blocks, den = bucket_weights(unit, valid)
    half = width_l // chunks
    outs = []
    scale = None
    for c in range(chunks):
        cols = slice(c * half, (c + 1) * half)
        num1 = weighted_sums(blocks, feats0[:, cols])
        if c == 0:
            packed = jnp.concatenate(
                [
                    num1.reshape(groups, slot * half),
                    jnp.pad(den.reshape(groups, slot), ((0, 0), (0, 128 - slot))),
                ],
                axis=1,
            )
            back = exchange(packed)
            back_num = back[:, : slot * half].reshape(groups * slot, half)
            back_den = back[:, slot * half : slot * half + slot].reshape(groups * slot)
            row_num = back_num[target]
            row_den = back_den[target]
            other_num, other_den = other_core((row_num, row_den))
            total_den = row_den + other_den
            scale = (1.0 + total_den)[:, None]
        else:
            back_num = exchange(num1.reshape(groups, slot, half)).reshape(groups * slot, half)
            row_num = back_num[target]
            other_num = other_core(row_num)
        total_num = row_num + other_num
        first = (1.0 - alpha_mix) * prior[:, cols] + alpha_mix * total_num / scale
        feats1 = exchange(place(first.astype(jnp.bfloat16)).reshape(groups, slot, -1))
        num2 = weighted_sums(blocks, feats1.reshape(groups * slot, -1))
        back2 = exchange(num2.reshape(groups, slot, -1)).reshape(groups * slot, -1)
        row_num2 = back2[target]
        total_num2 = row_num2 + other_core(row_num2)
        outs.append((1.0 - alpha_mix) * prior[:, cols] + alpha_mix * total_num2 / scale)
    return jnp.concatenate(outs, axis=1)


def solution(mesh):
    return jax.shard_map(
        body,
        mesh=mesh,
        in_specs=(P("gx", None), P("gx", None), P("ta", "gx", None)),
        out_specs=P("gx", None),
        check_vma=False,
    )
```

```python
import jax
import jax.numpy as jnp
from jax import lax
from jax.experimental import pallas as pl
from jax.experimental.pallas import tpu as pltpu
from jax.sharding import PartitionSpec as P

CAP = 2048
PAD_MARK = -1024.0


sharpness = 8.0
alpha_mix = 0.8


def normalize(embeds):
    wide = embeds.astype(jnp.float32)
    return (wide * lax.rsqrt(jnp.sum(wide * wide, axis=1, keepdims=True) + 1e-06)).astype(
        jnp.bfloat16
    )


def a2a_kernel(x_ref, o_ref, send_sem, recv_sem, local_sem):
    n = x_ref.shape[0]
    me = lax.axis_index("gx")
    core = lax.axis_index("ta")
    mesh_ids = pl.DeviceIdType.MESH
    barrier = pltpu.get_barrier_semaphore()

    def greet(i, carry):
        peer = lax.rem(me + 1 + i, n)
        pl.semaphore_signal(barrier, 1, device_id=(peer, core), device_id_type=mesh_ids)
        return carry

    lax.fori_loop(0, n - 1, greet, 0)
    pl.semaphore_wait(barrier, n - 1)
    local = pltpu.make_async_copy(x_ref.at[me], o_ref.at[me], local_sem)
    local.start()

    def copy_with(peer, block_from, block_to):
        return pltpu.make_async_remote_copy(
            x_ref.at[block_from],
            o_ref.at[block_to],
            send_sem.at[block_from],
            recv_sem.at[block_to],
            device_id=(peer, core),
            device_id_type=mesh_ids,
        )

    def send(i, carry):
        peer = lax.rem(me + 1 + i, n)
        copy_with(peer, peer, me).start()
        return carry

    lax.fori_loop(0, n - 1, send, 0)

    def finish(i, carry):
        peer = lax.rem(me + 1 + i, n)
        copy_with(peer, peer, me).wait_send()
        copy_with(peer, peer, peer).wait_recv()
        return carry

    lax.fori_loop(0, n - 1, finish, 0)
    local.wait()


def all_to_all(x, collective_id):
    return pl.pallas_call(
        a2a_kernel,
        out_shape=jax.ShapeDtypeStruct(x.shape, x.dtype),
        in_specs=[pl.BlockSpec(memory_space=pl.ANY)],
        out_specs=pl.BlockSpec(memory_space=pl.ANY),
        scratch_shapes=[
            pltpu.SemaphoreType.DMA((x.shape[0],)),
            pltpu.SemaphoreType.DMA((x.shape[0],)),
            pltpu.SemaphoreType.DMA(()),
        ],
        compiler_params=pltpu.CompilerParams(collective_id=collective_id, has_side_effects=True),
    )(x)


def bucket_weights(unit, valid):
    cap = unit.shape[0]
    block = min(512, cap)
    cols = jnp.arange(cap)
    blocks = []
    dens = []
    for start in range(0, cap, block):
        gram = lax.dot_general(
            unit[start : start + block],
            unit,
            (((1,), (1,)), ((), ())),
            preferred_element_type=jnp.float32,
        )
        keep = valid[None, :] * (cols[None, :] != (start + jnp.arange(block))[:, None]).astype(
            jnp.float32
        )
        weights = (jnp.exp(sharpness * gram) * keep).astype(jnp.bfloat16)
        blocks.append(weights)
        dens.append(jnp.sum(weights.astype(jnp.float32), axis=1))
    return blocks, jnp.concatenate(dens, axis=0)


def weighted_sums(blocks, feats):
    return jnp.concatenate(
        [jnp.dot(w, feats, preferred_element_type=jnp.float32) for w in blocks], axis=0
    )


def body(embeddings, labels, bucket_ids):
    groups = lax.axis_size("gx")
    rows = embeddings.shape[0]
    slot = CAP // groups
    width_l = labels.shape[1]
    ids = bucket_ids[0, :, 0]
    pos = jnp.arange(rows, dtype=jnp.int32)
    same = (ids[:, None] == ids[None, :]) & (pos[None, :] < pos[:, None])
    rank = jnp.sum(same.astype(jnp.int32), axis=1)
    target = ids * slot + rank
    slots = jnp.arange(groups * slot, dtype=jnp.int32)
    place_mat = (target[None, :] == slots[:, None]).astype(jnp.bfloat16)
    occupied = jnp.sum(place_mat.astype(jnp.float32), axis=1) > 0.5
    prior = labels.astype(jnp.float32)

    def place(payload):
        return jnp.dot(place_mat, payload, preferred_element_type=jnp.float32).astype(payload.dtype)

    calls = []

    def exchange(buffer):
        calls.append(None)
        return all_to_all(buffer, len(calls) - 1)

    def other_core(values):
        return lax.ppermute(values, "ta", perm=[(0, 1), (1, 0)])

    unit_here = normalize(embeddings)
    placed = place(jnp.concatenate([unit_here, labels], axis=1))
    mark = jnp.where(occupied, placed[:, unit_here.shape[1]], PAD_MARK)
    placed = placed.at[:, unit_here.shape[1]].set(mark.astype(jnp.bfloat16))
    got = exchange(placed.reshape(groups, slot, -1)).reshape(groups * slot, -1)
    unit = got[:, : unit_here.shape[1]]
    feats0 = got[:, unit_here.shape[1] :]
    valid = (feats0[:, 0].astype(jnp.float32) > PAD_MARK * 0.5).astype(jnp.float32)

    blocks, den = bucket_weights(unit, valid)
    num1 = weighted_sums(blocks, feats0)

    packed = jnp.concatenate(
        [
            num1.reshape(groups, slot * width_l),
            jnp.pad(den.reshape(groups, slot), ((0, 0), (0, 128 - slot))),
        ],
        axis=1,
    )
    back = exchange(packed)
    back_num = back[:, : slot * width_l].reshape(groups * slot, width_l)
    back_den = back[:, slot * width_l : slot * width_l + slot].reshape(groups * slot)
    row_num = back_num[target]
    row_den = back_den[target]
    other_num, other_den = other_core((row_num, row_den))
    total_num = row_num + other_num
    total_den = row_den + other_den
    scale = (1.0 + total_den)[:, None]
    first = (1.0 - alpha_mix) * prior + alpha_mix * total_num / scale

    feats1 = exchange(place(first.astype(jnp.bfloat16)).reshape(groups, slot, -1))
    num2 = weighted_sums(blocks, feats1.reshape(groups * slot, -1))
    back2 = exchange(num2.reshape(groups, slot, -1)).reshape(groups * slot, -1)
    row_num2 = back2[target]
    total_num2 = row_num2 + other_core(row_num2)
    return (1.0 - alpha_mix) * prior + alpha_mix * total_num2 / scale


def solution(mesh):
    return jax.shard_map(
        body,
        mesh=mesh,
        in_specs=(P("gx", None), P("gx", None), P("ta", "gx", None)),
        out_specs=P("gx", None),
        check_vma=False,
    )
```

```python
import jax
import jax.numpy as jnp
from jax import lax
from jax.experimental import pallas as pl
from jax.experimental.pallas import tpu as pltpu
from jax.sharding import PartitionSpec as P

CAP = 2048
PAD_MARK = -1024.0


sharpness = 8.0
alpha_mix = 0.8


def normalize(embeds):
    wide = embeds.astype(jnp.float32)
    return (wide * lax.rsqrt(jnp.sum(wide * wide, axis=1, keepdims=True) + 1e-06)).astype(
        jnp.bfloat16
    )


def a2a_kernel(x_ref, o_ref, send_sem, recv_sem, local_sem):
    n = x_ref.shape[0]
    me = lax.axis_index("gx")
    core = lax.axis_index("ta")
    mesh_ids = pl.DeviceIdType.MESH
    barrier = pltpu.get_barrier_semaphore()

    def greet(i, carry):
        peer = lax.rem(me + 1 + i, n)
        pl.semaphore_signal(barrier, 1, device_id=(peer, core), device_id_type=mesh_ids)
        return carry

    lax.fori_loop(0, n - 1, greet, 0)
    pl.semaphore_wait(barrier, n - 1)
    local = pltpu.make_async_copy(x_ref.at[me], o_ref.at[me], local_sem)
    local.start()

    def copy_with(peer, block_from, block_to):
        return pltpu.make_async_remote_copy(
            x_ref.at[block_from],
            o_ref.at[block_to],
            send_sem.at[block_from],
            recv_sem.at[block_to],
            device_id=(peer, core),
            device_id_type=mesh_ids,
        )

    def send(i, carry):
        peer = lax.rem(me + 1 + i, n)
        copy_with(peer, peer, me).start()
        return carry

    lax.fori_loop(0, n - 1, send, 0)

    def finish(i, carry):
        peer = lax.rem(me + 1 + i, n)
        copy_with(peer, peer, me).wait_send()
        copy_with(peer, peer, peer).wait_recv()
        return carry

    lax.fori_loop(0, n - 1, finish, 0)
    local.wait()


def all_to_all(x, collective_id):
    return pl.pallas_call(
        a2a_kernel,
        out_shape=jax.ShapeDtypeStruct(x.shape, x.dtype),
        in_specs=[pl.BlockSpec(memory_space=pl.ANY)],
        out_specs=pl.BlockSpec(memory_space=pl.ANY),
        scratch_shapes=[
            pltpu.SemaphoreType.DMA((x.shape[0],)),
            pltpu.SemaphoreType.DMA((x.shape[0],)),
            pltpu.SemaphoreType.DMA(()),
        ],
        compiler_params=pltpu.CompilerParams(collective_id=collective_id, has_side_effects=True),
    )(x)


def bucket_weights(unit, valid):
    cap = unit.shape[0]
    block = min(512, cap)
    cols = jnp.arange(cap)
    blocks = []
    dens = []
    for start in range(0, cap, block):
        gram = lax.dot_general(
            unit[start : start + block],
            unit,
            (((1,), (1,)), ((), ())),
            preferred_element_type=jnp.float32,
        )
        keep = valid[None, :] * (cols[None, :] != (start + jnp.arange(block))[:, None]).astype(
            jnp.float32
        )
        weights = (jnp.exp(sharpness * gram) * keep).astype(jnp.bfloat16)
        blocks.append(weights)
        dens.append(jnp.sum(weights.astype(jnp.float32), axis=1))
    return blocks, jnp.concatenate(dens, axis=0)


def weighted_sums(blocks, feats):
    return jnp.concatenate(
        [jnp.dot(w, feats, preferred_element_type=jnp.float32) for w in blocks], axis=0
    )


def body(embeddings, labels, bucket_ids):
    groups = lax.axis_size("gx")
    rows = embeddings.shape[0]
    slot = CAP // groups
    width_l = labels.shape[1]
    ids = bucket_ids[0, :, 0]
    pos = jnp.arange(rows, dtype=jnp.int32)
    same = (ids[:, None] == ids[None, :]) & (pos[None, :] < pos[:, None])
    rank = jnp.sum(same.astype(jnp.int32), axis=1)
    target = ids * slot + rank
    slots = jnp.arange(groups * slot, dtype=jnp.int32)
    place_mat = (target[None, :] == slots[:, None]).astype(jnp.bfloat16)
    occupied = jnp.sum(place_mat.astype(jnp.float32), axis=1) > 0.5
    prior = labels.astype(jnp.float32)

    def place(payload):
        return jnp.dot(place_mat, payload, preferred_element_type=jnp.float32).astype(payload.dtype)

    def exchange(buffer):
        return lax.all_to_all(buffer, "gx", split_axis=0, concat_axis=0, tiled=True)

    def other_core(values):
        return lax.ppermute(values, "ta", perm=[(0, 1), (1, 0)])

    unit_here = normalize(embeddings)
    placed = place(jnp.concatenate([unit_here, labels], axis=1))
    column = lax.broadcasted_iota(jnp.int32, placed.shape, 1)
    pad_here = (column == unit_here.shape[1]) & ~occupied[:, None]
    placed = jnp.where(pad_here, jnp.bfloat16(PAD_MARK), placed)
    got = all_to_all(placed.reshape(groups, slot, -1), 0).reshape(groups * slot, -1)
    unit = got[:, : unit_here.shape[1]]
    feats0 = got[:, unit_here.shape[1] :]
    valid = (feats0[:, 0].astype(jnp.float32) > PAD_MARK * 0.5).astype(jnp.float32)

    blocks, den = bucket_weights(unit, valid)
    num1 = weighted_sums(blocks, feats0)

    packed = jnp.concatenate(
        [
            num1.reshape(groups, slot * width_l),
            jnp.pad(den.reshape(groups, slot), ((0, 0), (0, 128 - slot))),
        ],
        axis=1,
    )
    back = exchange(packed)
    back_num = back[:, : slot * width_l].reshape(groups * slot, width_l)
    back_den = back[:, slot * width_l : slot * width_l + slot].reshape(groups * slot)
    row_num = back_num[target]
    row_den = jnp.broadcast_to(back_den[:, None], (groups * slot, 128))[target][:, 0]
    other_num, other_den = other_core((row_num, row_den))
    total_num = row_num + other_num
    total_den = row_den + other_den
    scale = (1.0 + total_den)[:, None]
    first = (1.0 - alpha_mix) * prior + alpha_mix * total_num / scale

    feats1 = exchange(place(first.astype(jnp.bfloat16)).reshape(groups, slot, -1))
    num2 = weighted_sums(blocks, feats1.reshape(groups * slot, -1))
    back2 = exchange(num2.reshape(groups, slot, -1)).reshape(groups * slot, -1)
    row_num2 = back2[target]
    total_num2 = row_num2 + other_core(row_num2)
    return (1.0 - alpha_mix) * prior + alpha_mix * total_num2 / scale


def solution(mesh):
    return jax.shard_map(
        body,
        mesh=mesh,
        in_specs=(P("gx", None), P("gx", None), P("ta", "gx", None)),
        out_specs=P("gx", None),
        check_vma=False,
    )
```

```python
import functools

import jax
import jax.numpy as jnp
from jax import lax
from jax.experimental import pallas as pl
from jax.experimental.pallas import tpu as pltpu
from jax.sharding import PartitionSpec as P

CAP = 2048
PAD_MARK = -1024.0


sharpness = 8.0
alpha_mix = 0.8


def normalize(embeds):
    wide = embeds.astype(jnp.float32)
    return (wide * lax.rsqrt(jnp.sum(wide * wide, axis=1, keepdims=True) + 1e-06)).astype(
        jnp.bfloat16
    )


def a2a_kernel(count, *refs):
    x_refs = refs[:count]
    o_refs = refs[count : 2 * count]
    send_sem, recv_sem, local_sem = refs[2 * count :]
    n = x_refs[0].shape[0]
    me = lax.axis_index("gx")
    core = lax.axis_index("ta")
    mesh_ids = pl.DeviceIdType.MESH
    barrier = pltpu.get_barrier_semaphore()

    def greet(i, carry):
        peer = lax.rem(me + 1 + i, n)
        pl.semaphore_signal(barrier, 1, device_id=(peer, core), device_id_type=mesh_ids)
        return carry

    lax.fori_loop(0, n - 1, greet, 0)
    pl.semaphore_wait(barrier, n - 1)
    locals_ = [
        pltpu.make_async_copy(x.at[me], o.at[me], local_sem.at[k])
        for k, (x, o) in enumerate(zip(x_refs, o_refs))
    ]
    for local in locals_:
        local.start()

    def copy_with(k, peer, block_from, block_to):
        return pltpu.make_async_remote_copy(
            x_refs[k].at[block_from],
            o_refs[k].at[block_to],
            send_sem.at[k, block_from],
            recv_sem.at[k, block_to],
            device_id=(peer, core),
            device_id_type=mesh_ids,
        )

    def send(i, carry):
        peer = lax.rem(me + 1 + i, n)
        for k in range(count):
            copy_with(k, peer, peer, me).start()
        return carry

    lax.fori_loop(0, n - 1, send, 0)

    def finish(i, carry):
        peer = lax.rem(me + 1 + i, n)
        for k in range(count):
            copy_with(k, peer, peer, me).wait_send()
            copy_with(k, peer, peer, peer).wait_recv()
        return carry

    lax.fori_loop(0, n - 1, finish, 0)
    for local in locals_:
        local.wait()


def all_to_all(arrays, collective_id):
    count = len(arrays)
    n = arrays[0].shape[0]
    return pl.pallas_call(
        functools.partial(a2a_kernel, count),
        out_shape=[jax.ShapeDtypeStruct(x.shape, x.dtype) for x in arrays],
        in_specs=[pl.BlockSpec(memory_space=pl.ANY)] * count,
        out_specs=[pl.BlockSpec(memory_space=pl.ANY)] * count,
        scratch_shapes=[
            pltpu.SemaphoreType.DMA((count, n)),
            pltpu.SemaphoreType.DMA((count, n)),
            pltpu.SemaphoreType.DMA((count,)),
        ],
        compiler_params=pltpu.CompilerParams(collective_id=collective_id, has_side_effects=True),
    )(*arrays)


def bucket_weights(unit, valid):
    cap = unit.shape[0]
    block = min(512, cap)
    cols = jnp.arange(cap)
    blocks = []
    dens = []
    for start in range(0, cap, block):
        gram = lax.dot_general(
            unit[start : start + block],
            unit,
            (((1,), (1,)), ((), ())),
            preferred_element_type=jnp.float32,
        )
        keep = valid[None, :] * (cols[None, :] != (start + jnp.arange(block))[:, None]).astype(
            jnp.float32
        )
        weights = (jnp.exp(sharpness * gram) * keep).astype(jnp.bfloat16)
        blocks.append(weights)
        dens.append(jnp.sum(weights.astype(jnp.float32), axis=1))
    return blocks, jnp.concatenate(dens, axis=0)


def weighted_sums(blocks, feats):
    return jnp.concatenate(
        [jnp.dot(w, feats, preferred_element_type=jnp.float32) for w in blocks], axis=0
    )


def body(embeddings, labels, bucket_ids):
    groups = lax.axis_size("gx")
    rows = embeddings.shape[0]
    slot = CAP // groups
    width_l = labels.shape[1]
    ids = bucket_ids[0, :, 0]
    pos = jnp.arange(rows, dtype=jnp.int32)
    same = (ids[:, None] == ids[None, :]) & (pos[None, :] < pos[:, None])
    rank = jnp.sum(same.astype(jnp.int32), axis=1)
    target = ids * slot + rank
    slots = jnp.arange(groups * slot, dtype=jnp.int32)
    place_mat = (target[None, :] == slots[:, None]).astype(jnp.bfloat16)
    occupied = jnp.sum(place_mat.astype(jnp.float32), axis=1) > 0.5
    prior = labels.astype(jnp.float32)

    def place(payload):
        return jnp.dot(place_mat, payload, preferred_element_type=jnp.float32).astype(payload.dtype)

    def exchange(buffer):
        return lax.all_to_all(buffer, "gx", split_axis=0, concat_axis=0, tiled=True)

    def other_core(values):
        return lax.ppermute(values, "ta", perm=[(0, 1), (1, 0)])

    unit_here = normalize(embeddings)
    placed = place(jnp.concatenate([unit_here, labels], axis=1))
    column = lax.broadcasted_iota(jnp.int32, placed.shape, 1)
    pad_here = (column == unit_here.shape[1]) & ~occupied[:, None]
    placed = jnp.where(pad_here, jnp.bfloat16(PAD_MARK), placed)
    got = exchange(placed.reshape(groups, slot, -1)).reshape(groups * slot, -1)
    unit = got[:, : unit_here.shape[1]]
    feats0 = got[:, unit_here.shape[1] :]
    valid = (feats0[:, 0].astype(jnp.float32) > PAD_MARK * 0.5).astype(jnp.float32)

    blocks, den = bucket_weights(unit, valid)
    num1 = weighted_sums(blocks, feats0)

    back_num, back_den = all_to_all([num1.reshape(groups, slot, width_l), den.reshape(groups, slot)], 0)
    back_num = back_num.reshape(groups * slot, width_l)
    back_den = back_den.reshape(groups * slot)
    row_num = back_num[target]
    row_den = jnp.broadcast_to(back_den[:, None], (groups * slot, 128))[target][:, 0]
    other_num, other_den = other_core((row_num, row_den))
    total_num = row_num + other_num
    total_den = row_den + other_den
    scale = (1.0 + total_den)[:, None]
    first = (1.0 - alpha_mix) * prior + alpha_mix * total_num / scale

    feats1 = exchange(place(first.astype(jnp.bfloat16)).reshape(groups, slot, -1))
    num2 = weighted_sums(blocks, feats1.reshape(groups * slot, -1))
    back2 = exchange(num2.reshape(groups, slot, -1)).reshape(groups * slot, -1)
    row_num2 = back2[target]
    total_num2 = row_num2 + other_core(row_num2)
    return (1.0 - alpha_mix) * prior + alpha_mix * total_num2 / scale


def solution(mesh):
    return jax.shard_map(
        body,
        mesh=mesh,
        in_specs=(P("gx", None), P("gx", None), P("ta", "gx", None)),
        out_specs=P("gx", None),
        check_vma=False,
    )
```

```python
import functools

import jax
import jax.numpy as jnp
from jax import lax
from jax.experimental import pallas as pl
from jax.experimental.pallas import tpu as pltpu
from jax.sharding import PartitionSpec as P

CAP = 2048
PAD_MARK = -1024.0


sharpness = 8.0
alpha_mix = 0.8


def normalize(embeds):
    wide = embeds.astype(jnp.float32)
    return (wide * lax.rsqrt(jnp.sum(wide * wide, axis=1, keepdims=True) + 1e-06)).astype(
        jnp.bfloat16
    )


def a2a_kernel(count, *refs):
    x_refs = refs[:count]
    o_refs = refs[count : 2 * count]
    send_sem, recv_sem, local_sem = refs[2 * count :]
    n = x_refs[0].shape[0]
    me = lax.axis_index("gx")
    core = lax.axis_index("ta")
    mesh_ids = pl.DeviceIdType.MESH
    barrier = pltpu.get_barrier_semaphore()

    def greet(i, carry):
        peer = lax.rem(me + 1 + i, n)
        pl.semaphore_signal(barrier, 1, device_id=(peer, core), device_id_type=mesh_ids)
        return carry

    lax.fori_loop(0, n - 1, greet, 0)
    pl.semaphore_wait(barrier, n - 1)
    locals_ = [
        pltpu.make_async_copy(x.at[me], o.at[me], local_sem.at[k])
        for k, (x, o) in enumerate(zip(x_refs, o_refs))
    ]
    for local in locals_:
        local.start()

    def copy_with(k, peer, block_from, block_to):
        return pltpu.make_async_remote_copy(
            x_refs[k].at[block_from],
            o_refs[k].at[block_to],
            send_sem.at[k, block_from],
            recv_sem.at[k, block_to],
            device_id=(peer, core),
            device_id_type=mesh_ids,
        )

    def send(i, carry):
        peer = lax.rem(me + 1 + i, n)
        for k in range(count):
            copy_with(k, peer, peer, me).start()
        return carry

    lax.fori_loop(0, n - 1, send, 0)

    def finish(i, carry):
        peer = lax.rem(me + 1 + i, n)
        for k in range(count):
            copy_with(k, peer, peer, me).wait_send()
            copy_with(k, peer, peer, peer).wait_recv()
        return carry

    lax.fori_loop(0, n - 1, finish, 0)
    for local in locals_:
        local.wait()


def all_to_all(arrays, collective_id):
    count = len(arrays)
    n = arrays[0].shape[0]
    return pl.pallas_call(
        functools.partial(a2a_kernel, count),
        out_shape=[jax.ShapeDtypeStruct(x.shape, x.dtype) for x in arrays],
        in_specs=[pl.BlockSpec(memory_space=pl.ANY)] * count,
        out_specs=[pl.BlockSpec(memory_space=pl.ANY)] * count,
        scratch_shapes=[
            pltpu.SemaphoreType.DMA((count, n)),
            pltpu.SemaphoreType.DMA((count, n)),
            pltpu.SemaphoreType.DMA((count,)),
        ],
        compiler_params=pltpu.CompilerParams(collective_id=collective_id, has_side_effects=True),
    )(*arrays)


def bucket_weights(unit, valid):
    cap = unit.shape[0]
    block = cap
    cols = jnp.arange(cap)
    blocks = []
    dens = []
    for start in range(0, cap, block):
        gram = lax.dot_general(
            unit[start : start + block],
            unit,
            (((1,), (1,)), ((), ())),
            preferred_element_type=jnp.float32,
        )
        keep = valid[None, :] * (cols[None, :] != (start + jnp.arange(block))[:, None]).astype(
            jnp.float32
        )
        weights = (jnp.exp(sharpness * gram) * keep).astype(jnp.bfloat16)
        blocks.append(weights)
        dens.append(jnp.sum(weights.astype(jnp.float32), axis=1))
    return blocks, jnp.concatenate(dens, axis=0)


def weighted_sums(blocks, feats):
    return jnp.concatenate(
        [jnp.dot(w, feats, preferred_element_type=jnp.float32) for w in blocks], axis=0
    )


def body(embeddings, labels, bucket_ids):
    groups = lax.axis_size("gx")
    rows = embeddings.shape[0]
    slot = CAP // groups
    width_l = labels.shape[1]
    ids = bucket_ids[0, :, 0]
    pos = jnp.arange(rows, dtype=jnp.int32)
    same = (ids[:, None] == ids[None, :]) & (pos[None, :] < pos[:, None])
    rank = jnp.sum(same.astype(jnp.int32), axis=1)
    target = ids * slot + rank
    slots = jnp.arange(groups * slot, dtype=jnp.int32)
    place_mat = (target[None, :] == slots[:, None]).astype(jnp.bfloat16)
    occupied = jnp.sum(place_mat.astype(jnp.float32), axis=1) > 0.5
    prior = labels.astype(jnp.float32)

    def place(payload):
        return jnp.dot(place_mat, payload, preferred_element_type=jnp.float32).astype(payload.dtype)

    def exchange(buffer):
        return lax.all_to_all(buffer, "gx", split_axis=0, concat_axis=0, tiled=True)

    def other_core(values):
        return lax.ppermute(values, "ta", perm=[(0, 1), (1, 0)])

    unit_here = normalize(embeddings)
    placed = place(jnp.concatenate([unit_here, labels], axis=1))
    column = lax.broadcasted_iota(jnp.int32, placed.shape, 1)
    pad_here = (column == unit_here.shape[1]) & ~occupied[:, None]
    placed = jnp.where(pad_here, jnp.bfloat16(PAD_MARK), placed)
    got = exchange(placed.reshape(groups, slot, -1)).reshape(groups * slot, -1)
    unit = got[:, : unit_here.shape[1]]
    feats0 = got[:, unit_here.shape[1] :]
    valid = (feats0[:, 0].astype(jnp.float32) > PAD_MARK * 0.5).astype(jnp.float32)

    blocks, den = bucket_weights(unit, valid)
    num1 = weighted_sums(blocks, feats0)

    back_num, back_den = all_to_all([num1.reshape(groups, slot, width_l), den.reshape(groups, slot)], 0)
    back_num = back_num.reshape(groups * slot, width_l)
    back_den = back_den.reshape(groups * slot)
    row_num = back_num[target]
    row_den = jnp.broadcast_to(back_den[:, None], (groups * slot, 128))[target][:, 0]
    other_num, other_den = other_core((row_num, row_den))
    total_num = row_num + other_num
    total_den = row_den + other_den
    scale = (1.0 + total_den)[:, None]
    first = (1.0 - alpha_mix) * prior + alpha_mix * total_num / scale

    feats1 = exchange(place(first.astype(jnp.bfloat16)).reshape(groups, slot, -1))
    num2 = weighted_sums(blocks, feats1.reshape(groups * slot, -1))
    back2 = exchange(num2.reshape(groups, slot, -1)).reshape(groups * slot, -1)
    row_num2 = back2[target]
    total_num2 = row_num2 + other_core(row_num2)
    return (1.0 - alpha_mix) * prior + alpha_mix * total_num2 / scale


def solution(mesh):
    return jax.shard_map(
        body,
        mesh=mesh,
        in_specs=(P("gx", None), P("gx", None), P("ta", "gx", None)),
        out_specs=P("gx", None),
        check_vma=False,
    )
```

```python
import functools

import jax
import jax.numpy as jnp
from jax import lax
from jax.experimental import pallas as pl
from jax.experimental.pallas import tpu as pltpu
from jax.sharding import PartitionSpec as P

CAP = 2048
PAD_MARK = -1024.0


sharpness = 8.0
alpha_mix = 0.8


def normalize(embeds):
    wide = embeds.astype(jnp.float32)
    return (wide * lax.rsqrt(jnp.sum(wide * wide, axis=1, keepdims=True) + 1e-06)).astype(
        jnp.bfloat16
    )


def a2a_kernel(count, *refs):
    x_refs = refs[:count]
    o_refs = refs[count : 2 * count]
    send_sem, recv_sem, local_sem = refs[2 * count :]
    n = x_refs[0].shape[0]
    me = lax.axis_index("gx")
    core = lax.axis_index("ta")
    mesh_ids = pl.DeviceIdType.MESH
    barrier = pltpu.get_barrier_semaphore()

    def greet(i, carry):
        peer = lax.rem(me + 1 + i, n)
        pl.semaphore_signal(barrier, 1, device_id=(peer, core), device_id_type=mesh_ids)
        return carry

    lax.fori_loop(0, n - 1, greet, 0)
    pl.semaphore_wait(barrier, n - 1)
    locals_ = [
        pltpu.make_async_copy(x.at[me], o.at[me], local_sem.at[k])
        for k, (x, o) in enumerate(zip(x_refs, o_refs))
    ]
    for local in locals_:
        local.start()

    def copy_with(k, peer, block_from, block_to):
        return pltpu.make_async_remote_copy(
            x_refs[k].at[block_from],
            o_refs[k].at[block_to],
            send_sem.at[k, block_from],
            recv_sem.at[k, block_to],
            device_id=(peer, core),
            device_id_type=mesh_ids,
        )

    def send(i, carry):
        peer = lax.rem(me + 1 + i, n)
        for k in range(count):
            copy_with(k, peer, peer, me).start()
        return carry

    lax.fori_loop(0, n - 1, send, 0)

    def finish(i, carry):
        peer = lax.rem(me + 1 + i, n)
        for k in range(count):
            copy_with(k, peer, peer, me).wait_send()
            copy_with(k, peer, peer, peer).wait_recv()
        return carry

    lax.fori_loop(0, n - 1, finish, 0)
    for local in locals_:
        local.wait()


def all_to_all(arrays, collective_id):
    count = len(arrays)
    n = arrays[0].shape[0]
    return pl.pallas_call(
        functools.partial(a2a_kernel, count),
        out_shape=[jax.ShapeDtypeStruct(x.shape, x.dtype) for x in arrays],
        in_specs=[pl.BlockSpec(memory_space=pl.ANY)] * count,
        out_specs=[pl.BlockSpec(memory_space=pl.ANY)] * count,
        scratch_shapes=[
            pltpu.SemaphoreType.DMA((count, n)),
            pltpu.SemaphoreType.DMA((count, n)),
            pltpu.SemaphoreType.DMA((count,)),
        ],
        compiler_params=pltpu.CompilerParams(collective_id=collective_id, has_side_effects=True),
    )(*arrays)


def bucket_weights(unit, valid):
    cap = unit.shape[0]
    block = cap
    cols = jnp.arange(cap)
    blocks = []
    dens = []
    for start in range(0, cap, block):
        gram = lax.dot_general(
            unit[start : start + block],
            unit,
            (((1,), (1,)), ((), ())),
            preferred_element_type=jnp.float32,
        )
        keep = valid[None, :] * (cols[None, :] != (start + jnp.arange(block))[:, None]).astype(
            jnp.float32
        )
        weights = (jnp.exp(sharpness * gram) * keep).astype(jnp.bfloat16)
        blocks.append(weights)
        dens.append(jnp.sum(weights.astype(jnp.float32), axis=1))
    return blocks, jnp.concatenate(dens, axis=0)


def weighted_sums(blocks, feats):
    return jnp.concatenate(
        [jnp.dot(w, feats, preferred_element_type=jnp.float32) for w in blocks], axis=0
    )


def body(embeddings, labels, bucket_ids):
    groups = lax.axis_size("gx")
    rows = embeddings.shape[0]
    slot = CAP // groups
    width_l = labels.shape[1]
    ids = bucket_ids[0, :, 0]
    pos = jnp.arange(rows, dtype=jnp.int32)
    same = (ids[:, None] == ids[None, :]) & (pos[None, :] < pos[:, None])
    rank = jnp.sum(same.astype(jnp.int32), axis=1)
    target = ids * slot + rank
    slots = jnp.arange(groups * slot, dtype=jnp.int32)
    place_mat = (target[None, :] == slots[:, None]).astype(jnp.bfloat16)
    occupied = jnp.sum(place_mat.astype(jnp.float32), axis=1) > 0.5
    prior = labels.astype(jnp.float32)

    def place(payload):
        return jnp.dot(place_mat, payload, preferred_element_type=jnp.float32).astype(payload.dtype)

    def exchange(buffer):
        return lax.all_to_all(buffer, "gx", split_axis=0, concat_axis=0, tiled=True)

    def other_core(values):
        return lax.ppermute(values, "ta", perm=[(0, 1), (1, 0)])

    unit_here = normalize(embeddings)
    placed_l = place(labels)
    column = lax.broadcasted_iota(jnp.int32, placed_l.shape, 1)
    placed_l = jnp.where((column == 0) & ~occupied[:, None], jnp.bfloat16(PAD_MARK), placed_l)
    unit, feats0 = all_to_all(
        [place(unit_here).reshape(groups, slot, -1), placed_l.reshape(groups, slot, -1)], 1
    )
    unit = unit.reshape(groups * slot, -1)
    feats0 = feats0.reshape(groups * slot, -1)
    valid = (feats0[:, 0].astype(jnp.float32) > PAD_MARK * 0.5).astype(jnp.float32)

    blocks, den = bucket_weights(unit, valid)
    num1 = weighted_sums(blocks, feats0)

    back_num, back_den = all_to_all([num1.reshape(groups, slot, width_l), den.reshape(groups, slot)], 0)
    back_num = back_num.reshape(groups * slot, width_l)
    back_den = back_den.reshape(groups * slot)
    row_num = back_num[target]
    row_den = jnp.broadcast_to(back_den[:, None], (groups * slot, 128))[target][:, 0]
    other_num, other_den = other_core((row_num, row_den))
    total_num = row_num + other_num
    total_den = row_den + other_den
    scale = (1.0 + total_den)[:, None]
    first = (1.0 - alpha_mix) * prior + alpha_mix * total_num / scale

    (feats1,) = all_to_all([place(first.astype(jnp.bfloat16)).reshape(groups, slot, -1)], 2)
    num2 = weighted_sums(blocks, feats1.reshape(groups * slot, -1))
    back2 = exchange(num2.reshape(groups, slot, -1)).reshape(groups * slot, -1)
    row_num2 = back2[target]
    total_num2 = row_num2 + other_core(row_num2)
    return (1.0 - alpha_mix) * prior + alpha_mix * total_num2 / scale


def solution(mesh):
    return jax.shard_map(
        body,
        mesh=mesh,
        in_specs=(P("gx", None), P("gx", None), P("ta", "gx", None)),
        out_specs=P("gx", None),
        check_vma=False,
    )
```

```python
import functools

import jax
import jax.numpy as jnp
from jax import lax
from jax.experimental import pallas as pl
from jax.experimental.pallas import tpu as pltpu
from jax.sharding import PartitionSpec as P

CAP = 2048
PAD_MARK = -1024.0


sharpness = 8.0
alpha_mix = 0.8


def normalize(embeds):
    wide = embeds.astype(jnp.float32)
    return (wide * lax.rsqrt(jnp.sum(wide * wide, axis=1, keepdims=True) + 1e-06)).astype(
        jnp.bfloat16
    )


def a2a_kernel(count, *refs):
    x_refs = refs[:count]
    o_refs = refs[count : 2 * count]
    send_sem, recv_sem, local_sem = refs[2 * count :]
    n = x_refs[0].shape[0]
    me = lax.axis_index("gx")
    core = lax.axis_index("ta")
    mesh_ids = pl.DeviceIdType.MESH
    barrier = pltpu.get_barrier_semaphore()

    def greet(i, carry):
        peer = lax.rem(me + 1 + i, n)
        pl.semaphore_signal(barrier, 1, device_id=(peer, core), device_id_type=mesh_ids)
        return carry

    lax.fori_loop(0, n - 1, greet, 0)
    pl.semaphore_wait(barrier, n - 1)
    locals_ = [
        pltpu.make_async_copy(x.at[me], o.at[me], local_sem.at[k])
        for k, (x, o) in enumerate(zip(x_refs, o_refs))
    ]
    for local in locals_:
        local.start()

    def copy_with(k, peer, block_from, block_to):
        return pltpu.make_async_remote_copy(
            x_refs[k].at[block_from],
            o_refs[k].at[block_to],
            send_sem.at[k, block_from],
            recv_sem.at[k, block_to],
            device_id=(peer, core),
            device_id_type=mesh_ids,
        )

    def send(i, carry):
        peer = lax.rem(me + 1 + i, n)
        for k in range(count):
            copy_with(k, peer, peer, me).start()
        return carry

    lax.fori_loop(0, n - 1, send, 0)

    def finish(i, carry):
        peer = lax.rem(me + 1 + i, n)
        for k in range(count):
            copy_with(k, peer, peer, me).wait_send()
            copy_with(k, peer, peer, peer).wait_recv()
        return carry

    lax.fori_loop(0, n - 1, finish, 0)
    for local in locals_:
        local.wait()


def all_to_all(arrays, collective_id):
    count = len(arrays)
    n = arrays[0].shape[0]
    return pl.pallas_call(
        functools.partial(a2a_kernel, count),
        out_shape=[jax.ShapeDtypeStruct(x.shape, x.dtype) for x in arrays],
        in_specs=[pl.BlockSpec(memory_space=pl.ANY)] * count,
        out_specs=[pl.BlockSpec(memory_space=pl.ANY)] * count,
        scratch_shapes=[
            pltpu.SemaphoreType.DMA((count, n)),
            pltpu.SemaphoreType.DMA((count, n)),
            pltpu.SemaphoreType.DMA((count,)),
        ],
        compiler_params=pltpu.CompilerParams(collective_id=collective_id, has_side_effects=True),
    )(*arrays)


def bucket_weights(unit, valid):
    cap = unit.shape[0]
    block = cap
    cols = jnp.arange(cap)
    blocks = []
    dens = []
    for start in range(0, cap, block):
        gram = lax.dot_general(
            unit[start : start + block],
            unit,
            (((1,), (1,)), ((), ())),
            preferred_element_type=jnp.float32,
        )
        keep = valid[None, :] * (cols[None, :] != (start + jnp.arange(block))[:, None]).astype(
            jnp.float32
        )
        weights = (jnp.exp(sharpness * gram) * keep).astype(jnp.bfloat16)
        blocks.append(weights)
        dens.append(jnp.sum(weights.astype(jnp.float32), axis=1))
    return blocks, jnp.concatenate(dens, axis=0)


def weighted_sums(blocks, feats):
    return jnp.concatenate(
        [jnp.dot(w, feats, preferred_element_type=jnp.float32) for w in blocks], axis=0
    )


def body(embeddings, labels, bucket_ids):
    groups = lax.axis_size("gx")
    rows = embeddings.shape[0]
    slot = CAP // groups
    width_l = labels.shape[1]
    ids = bucket_ids[0, :, 0]
    pos = jnp.arange(rows, dtype=jnp.int32)
    same = (ids[:, None] == ids[None, :]) & (pos[None, :] < pos[:, None])
    rank = jnp.sum(same.astype(jnp.int32), axis=1)
    target = ids * slot + rank
    slots = jnp.arange(groups * slot, dtype=jnp.int32)
    place_mat = (target[None, :] == slots[:, None]).astype(jnp.bfloat16)
    occupied = jnp.sum(place_mat.astype(jnp.float32), axis=1) > 0.5
    prior = labels.astype(jnp.float32)

    def place(payload):
        return jnp.dot(place_mat, payload, preferred_element_type=jnp.float32).astype(payload.dtype)

    def exchange(buffer):
        return lax.all_to_all(buffer, "gx", split_axis=0, concat_axis=0, tiled=True)

    def other_core(values):
        return lax.ppermute(values, "ta", perm=[(0, 1), (1, 0)])

    unit_here = normalize(embeddings)
    placed = place(jnp.concatenate([unit_here, labels], axis=1))
    column = lax.broadcasted_iota(jnp.int32, placed.shape, 1)
    pad_here = (column == unit_here.shape[1]) & ~occupied[:, None]
    placed = jnp.where(pad_here, jnp.bfloat16(PAD_MARK), placed)
    got = exchange(placed.reshape(groups, slot, -1)).reshape(groups * slot, -1)
    unit = got[:, : unit_here.shape[1]]
    feats0 = got[:, unit_here.shape[1] :]
    valid = (feats0[:, 0].astype(jnp.float32) > PAD_MARK * 0.5).astype(jnp.float32)

    blocks, den = bucket_weights(unit, valid)
    num1 = weighted_sums(blocks, feats0)

    back_num, back_den = all_to_all([num1.reshape(groups, slot, width_l), den.reshape(groups, slot)], 0)
    back_num = back_num.reshape(groups * slot, width_l)
    back_den = back_den.reshape(groups * slot)
    row_num = back_num[target]
    row_den = jnp.sum(jnp.where(target[None, :] == slots[:, None], back_den[:, None], 0.0), axis=0)
    other_num, other_den = other_core((row_num, row_den))
    total_num = row_num + other_num
    total_den = row_den + other_den
    scale = (1.0 + total_den)[:, None]
    first = (1.0 - alpha_mix) * prior + alpha_mix * total_num / scale

    feats1 = exchange(place(first.astype(jnp.bfloat16)).reshape(groups, slot, -1))
    num2 = weighted_sums(blocks, feats1.reshape(groups * slot, -1))
    back2 = exchange(num2.reshape(groups, slot, -1)).reshape(groups * slot, -1)
    halves = []
    for part in range(2):
        rows_part = slice(part * (rows // 2), (part + 1) * (rows // 2))
        row_num2 = back2[target[rows_part]]
        total_num2 = row_num2 + other_core(row_num2)
        halves.append(
            (1.0 - alpha_mix) * prior[rows_part] + alpha_mix * total_num2 / scale[rows_part]
        )
    return jnp.concatenate(halves, axis=0)


def solution(mesh):
    return jax.shard_map(
        body,
        mesh=mesh,
        in_specs=(P("gx", None), P("gx", None), P("ta", "gx", None)),
        out_specs=P("gx", None),
        check_vma=False,
    )
```

```python
import functools

import jax
import jax.numpy as jnp
from jax import lax
from jax.experimental import pallas as pl
from jax.experimental.pallas import tpu as pltpu
from jax.sharding import PartitionSpec as P

CAP = 2048
PAD_MARK = -1024.0


sharpness = 8.0
alpha_mix = 0.8


def normalize(embeds):
    wide = embeds.astype(jnp.float32)
    return (wide * lax.rsqrt(jnp.sum(wide * wide, axis=1, keepdims=True) + 1e-06)).astype(
        jnp.bfloat16
    )


def a2a_kernel(count, *refs):
    x_refs = refs[:count]
    o_refs = refs[count : 2 * count]
    send_sem, recv_sem, local_sem = refs[2 * count :]
    n = x_refs[0].shape[0]
    me = lax.axis_index("gx")
    core = lax.axis_index("ta")
    mesh_ids = pl.DeviceIdType.MESH
    barrier = pltpu.get_barrier_semaphore()

    def greet(i, carry):
        peer = lax.rem(me + 1 + i, n)
        pl.semaphore_signal(barrier, 1, device_id=(peer, core), device_id_type=mesh_ids)
        return carry

    lax.fori_loop(0, n - 1, greet, 0)
    pl.semaphore_wait(barrier, n - 1)
    locals_ = [
        pltpu.make_async_copy(x.at[me], o.at[me], local_sem.at[k])
        for k, (x, o) in enumerate(zip(x_refs, o_refs))
    ]
    for local in locals_:
        local.start()

    def copy_with(k, peer, block_from, block_to):
        return pltpu.make_async_remote_copy(
            x_refs[k].at[block_from],
            o_refs[k].at[block_to],
            send_sem.at[k, block_from],
            recv_sem.at[k, block_to],
            device_id=(peer, core),
            device_id_type=mesh_ids,
        )

    def send(i, carry):
        peer = lax.rem(me + 1 + i, n)
        for k in range(count):
            copy_with(k, peer, peer, me).start()
        return carry

    lax.fori_loop(0, n - 1, send, 0)

    def finish(i, carry):
        peer = lax.rem(me + 1 + i, n)
        for k in range(count):
            copy_with(k, peer, peer, me).wait_send()
            copy_with(k, peer, peer, peer).wait_recv()
        return carry

    lax.fori_loop(0, n - 1, finish, 0)
    for local in locals_:
        local.wait()


def all_to_all(arrays, collective_id):
    count = len(arrays)
    n = arrays[0].shape[0]
    return pl.pallas_call(
        functools.partial(a2a_kernel, count),
        out_shape=[jax.ShapeDtypeStruct(x.shape, x.dtype) for x in arrays],
        in_specs=[pl.BlockSpec(memory_space=pl.ANY)] * count,
        out_specs=[pl.BlockSpec(memory_space=pl.ANY)] * count,
        scratch_shapes=[
            pltpu.SemaphoreType.DMA((count, n)),
            pltpu.SemaphoreType.DMA((count, n)),
            pltpu.SemaphoreType.DMA((count,)),
        ],
        compiler_params=pltpu.CompilerParams(collective_id=collective_id, has_side_effects=True),
    )(*arrays)


def bucket_weights(unit, valid):
    cap = unit.shape[0]
    block = cap
    cols = jnp.arange(cap)
    blocks = []
    dens = []
    for start in range(0, cap, block):
        gram = lax.dot_general(
            unit[start : start + block],
            unit,
            (((1,), (1,)), ((), ())),
            preferred_element_type=jnp.float32,
        )
        keep = valid[None, :] * (cols[None, :] != (start + jnp.arange(block))[:, None]).astype(
            jnp.float32
        )
        weights = (jnp.exp(sharpness * gram) * keep).astype(jnp.bfloat16)
        blocks.append(weights)
        dens.append(jnp.sum(weights.astype(jnp.float32), axis=1))
    return blocks, jnp.concatenate(dens, axis=0)


def weighted_sums(blocks, feats):
    return jnp.concatenate(
        [jnp.dot(w, feats, preferred_element_type=jnp.float32) for w in blocks], axis=0
    )


def body(embeddings, labels, bucket_ids):
    groups = lax.axis_size("gx")
    rows = embeddings.shape[0]
    slot = CAP // groups
    width_l = labels.shape[1]
    ids = bucket_ids[0, :, 0]
    pos = jnp.arange(rows, dtype=jnp.int32)
    same = (ids[:, None] == ids[None, :]) & (pos[None, :] < pos[:, None])
    rank = jnp.sum(same.astype(jnp.int32), axis=1)
    target = ids * slot + rank
    slots = jnp.arange(groups * slot, dtype=jnp.int32)
    place_mat = (target[None, :] == slots[:, None]).astype(jnp.bfloat16)
    occupied = jnp.sum(place_mat.astype(jnp.float32), axis=1) > 0.5
    prior = labels.astype(jnp.float32)

    def place(payload):
        return jnp.dot(place_mat, payload, preferred_element_type=jnp.float32).astype(payload.dtype)

    def exchange(buffer):
        return lax.all_to_all(buffer, "gx", split_axis=0, concat_axis=0, tiled=True)

    def other_core(values):
        return lax.ppermute(values, "ta", perm=[(0, 1), (1, 0)])

    unit_here = normalize(embeddings)
    placed = place(jnp.concatenate([unit_here, labels], axis=1))
    column = lax.broadcasted_iota(jnp.int32, placed.shape, 1)
    pad_here = (column == unit_here.shape[1]) & ~occupied[:, None]
    placed = jnp.where(pad_here, jnp.bfloat16(PAD_MARK), placed)
    (got,) = all_to_all([placed.reshape(groups, slot, -1)], 1)
    got = got.reshape(groups * slot, -1)
    unit = got[:, : unit_here.shape[1]]
    feats0 = got[:, unit_here.shape[1] :]
    valid = (feats0[:, 0].astype(jnp.float32) > PAD_MARK * 0.5).astype(jnp.float32)

    blocks, den = bucket_weights(unit, valid)
    num1 = weighted_sums(blocks, feats0)

    back_num, back_den = all_to_all([num1.reshape(groups, slot, width_l), den.reshape(groups, slot)], 0)
    back_num = back_num.reshape(groups * slot, width_l)
    back_den = back_den.reshape(groups * slot)
    row_num = back_num[target]
    row_den = jnp.sum(jnp.where(target[None, :] == slots[:, None], back_den[:, None], 0.0), axis=0)
    other_num, other_den = other_core((row_num, row_den))
    total_num = row_num + other_num
    total_den = row_den + other_den
    scale = (1.0 + total_den)[:, None]
    first = (1.0 - alpha_mix) * prior + alpha_mix * total_num / scale

    feats1 = exchange(place(first.astype(jnp.bfloat16)).reshape(groups, slot, -1))
    num2 = weighted_sums(blocks, feats1.reshape(groups * slot, -1))
    back2 = exchange(num2.reshape(groups, slot, -1)).reshape(groups * slot, -1)
    halves = []
    for part in range(2):
        rows_part = slice(part * (rows // 2), (part + 1) * (rows // 2))
        row_num2 = back2[target[rows_part]]
        total_num2 = row_num2 + other_core(row_num2)
        halves.append(
            (1.0 - alpha_mix) * prior[rows_part] + alpha_mix * total_num2 / scale[rows_part]
        )
    return jnp.concatenate(halves, axis=0)


def solution(mesh):
    return jax.shard_map(
        body,
        mesh=mesh,
        in_specs=(P("gx", None), P("gx", None), P("ta", "gx", None)),
        out_specs=P("gx", None),
        check_vma=False,
    )
```

```python
import functools

import jax
import jax.numpy as jnp
from jax import lax
from jax.experimental import pallas as pl
from jax.experimental.pallas import tpu as pltpu
from jax.sharding import PartitionSpec as P

CAP = 2048
PAD_MARK = -1024.0


sharpness = 8.0
alpha_mix = 0.8


def normalize(embeds):
    wide = embeds.astype(jnp.float32)
    return (wide * lax.rsqrt(jnp.sum(wide * wide, axis=1, keepdims=True) + 1e-06)).astype(
        jnp.bfloat16
    )


def a2a_kernel(count, *refs):
    x_refs = refs[:count]
    o_refs = refs[count : 2 * count]
    send_sem, recv_sem, local_sem = refs[2 * count :]
    n = x_refs[0].shape[0]
    me = lax.axis_index("gx")
    core = lax.axis_index("ta")
    mesh_ids = pl.DeviceIdType.MESH
    barrier = pltpu.get_barrier_semaphore()

    def greet(i, carry):
        peer = lax.rem(me + 1 + i, n)
        pl.semaphore_signal(barrier, 1, device_id=(peer, core), device_id_type=mesh_ids)
        return carry

    lax.fori_loop(0, n - 1, greet, 0)
    pl.semaphore_wait(barrier, n - 1)
    locals_ = [
        pltpu.make_async_copy(x.at[me], o.at[me], local_sem.at[k])
        for k, (x, o) in enumerate(zip(x_refs, o_refs))
    ]
    for local in locals_:
        local.start()

    def copy_with(k, peer, block_from, block_to):
        return pltpu.make_async_remote_copy(
            x_refs[k].at[block_from],
            o_refs[k].at[block_to],
            send_sem.at[k, block_from],
            recv_sem.at[k, block_to],
            device_id=(peer, core),
            device_id_type=mesh_ids,
        )

    def send(i, carry):
        peer = lax.rem(me + 1 + i, n)
        for k in range(count):
            copy_with(k, peer, peer, me).start()
        return carry

    lax.fori_loop(0, n - 1, send, 0)

    def finish(i, carry):
        peer = lax.rem(me + 1 + i, n)
        for k in range(count):
            copy_with(k, peer, peer, me).wait_send()
            copy_with(k, peer, peer, peer).wait_recv()
        return carry

    lax.fori_loop(0, n - 1, finish, 0)
    for local in locals_:
        local.wait()


def all_to_all(arrays, collective_id):
    count = len(arrays)
    n = arrays[0].shape[0]
    return pl.pallas_call(
        functools.partial(a2a_kernel, count),
        out_shape=[jax.ShapeDtypeStruct(x.shape, x.dtype) for x in arrays],
        in_specs=[pl.BlockSpec(memory_space=pl.ANY)] * count,
        out_specs=[pl.BlockSpec(memory_space=pl.ANY)] * count,
        scratch_shapes=[
            pltpu.SemaphoreType.DMA((count, n)),
            pltpu.SemaphoreType.DMA((count, n)),
            pltpu.SemaphoreType.DMA((count,)),
        ],
        compiler_params=pltpu.CompilerParams(collective_id=collective_id, has_side_effects=True),
    )(*arrays)


def weights_kernel(rows_ref, unit_ref, feats_ref, valid_ref, w_ref, den_ref, num_ref):
    block = rows_ref.shape[0]
    start = pl.program_id(0) * block
    gram = lax.dot_general(
        rows_ref[...],
        unit_ref[...],
        (((1,), (1,)), ((), ())),
        preferred_element_type=jnp.float32,
    )
    cols = lax.broadcasted_iota(jnp.int32, gram.shape, 1)
    rows = lax.broadcasted_iota(jnp.int32, gram.shape, 0) + start
    keep = jnp.where(cols != rows, valid_ref[...], 0.0)
    weights = (jnp.exp(sharpness * gram) * keep).astype(jnp.bfloat16)
    w_ref[...] = weights
    den_ref[...] = jnp.sum(weights.astype(jnp.float32), axis=1, keepdims=True)
    num_ref[...] = jnp.dot(weights, feats_ref[...], preferred_element_type=jnp.float32)


def bucket_round_one(unit, feats, valid, block=256):
    cap, width_e = unit.shape
    width_l = feats.shape[1]
    whole = lambda i: (0, 0)
    return pl.pallas_call(
        weights_kernel,
        grid=(cap // block,),
        out_shape=[
            jax.ShapeDtypeStruct((cap, cap), jnp.bfloat16),
            jax.ShapeDtypeStruct((cap, 1), jnp.float32),
            jax.ShapeDtypeStruct((cap, width_l), jnp.float32),
        ],
        in_specs=[
            pl.BlockSpec((block, width_e), lambda i: (i, 0)),
            pl.BlockSpec((cap, width_e), whole),
            pl.BlockSpec((cap, width_l), whole),
            pl.BlockSpec((1, cap), whole),
        ],
        out_specs=[
            pl.BlockSpec((block, cap), lambda i: (i, 0)),
            pl.BlockSpec((block, 1), lambda i: (i, 0)),
            pl.BlockSpec((block, width_l), lambda i: (i, 0)),
        ],
        cost_estimate=pl.CostEstimate(
            flops=2 * cap * cap * (width_e + width_l),
            transcendentals=cap * cap,
            bytes_accessed=2 * cap * (cap + width_e + width_l) + 4 * cap * (width_l + 2),
        ),
    )(unit, unit, feats, valid[None, :])


def body(embeddings, labels, bucket_ids):
    groups = lax.axis_size("gx")
    rows = embeddings.shape[0]
    slot = CAP // groups
    width_l = labels.shape[1]
    ids = bucket_ids[0, :, 0]
    pos = jnp.arange(rows, dtype=jnp.int32)
    same = (ids[:, None] == ids[None, :]) & (pos[None, :] < pos[:, None])
    rank = jnp.sum(same.astype(jnp.int32), axis=1)
    target = ids * slot + rank
    slots = jnp.arange(groups * slot, dtype=jnp.int32)
    place_mat = (target[None, :] == slots[:, None]).astype(jnp.bfloat16)
    occupied = jnp.sum(place_mat.astype(jnp.float32), axis=1) > 0.5
    prior = labels.astype(jnp.float32)

    def place(payload):
        return jnp.dot(place_mat, payload, preferred_element_type=jnp.float32).astype(payload.dtype)

    def exchange(buffer):
        return lax.all_to_all(buffer, "gx", split_axis=0, concat_axis=0, tiled=True)

    def other_core(values):
        return lax.ppermute(values, "ta", perm=[(0, 1), (1, 0)])

    unit_here = normalize(embeddings)
    placed = place(jnp.concatenate([unit_here, labels], axis=1))
    column = lax.broadcasted_iota(jnp.int32, placed.shape, 1)
    pad_here = (column == unit_here.shape[1]) & ~occupied[:, None]
    placed = jnp.where(pad_here, jnp.bfloat16(PAD_MARK), placed)
    got = exchange(placed.reshape(groups, slot, -1)).reshape(groups * slot, -1)
    unit = got[:, : unit_here.shape[1]]
    feats0 = got[:, unit_here.shape[1] :]
    valid = (feats0[:, 0].astype(jnp.float32) > PAD_MARK * 0.5).astype(jnp.float32)

    weights, den, num1 = bucket_round_one(unit, feats0, valid)

    back_num, back_den = all_to_all([num1.reshape(groups, slot, width_l), den.reshape(groups, slot)], 0)
    back_num = back_num.reshape(groups * slot, width_l)
    back_den = back_den.reshape(groups * slot)
    row_num = back_num[target]
    row_den = jnp.sum(jnp.where(target[None, :] == slots[:, None], back_den[:, None], 0.0), axis=0)
    other_num, other_den = other_core((row_num, row_den))
    total_num = row_num + other_num
    total_den = row_den + other_den
    scale = (1.0 + total_den)[:, None]
    first = (1.0 - alpha_mix) * prior + alpha_mix * total_num / scale

    feats1 = exchange(place(first.astype(jnp.bfloat16)).reshape(groups, slot, -1))
    num2 = jnp.dot(weights, feats1.reshape(groups * slot, -1), preferred_element_type=jnp.float32)
    back2 = exchange(num2.reshape(groups, slot, -1)).reshape(groups * slot, -1)
    halves = []
    for part in range(2):
        rows_part = slice(part * (rows // 2), (part + 1) * (rows // 2))
        row_num2 = back2[target[rows_part]]
        total_num2 = row_num2 + other_core(row_num2)
        halves.append(
            (1.0 - alpha_mix) * prior[rows_part] + alpha_mix * total_num2 / scale[rows_part]
        )
    return jnp.concatenate(halves, axis=0)


def solution(mesh):
    return jax.shard_map(
        body,
        mesh=mesh,
        in_specs=(P("gx", None), P("gx", None), P("ta", "gx", None)),
        out_specs=P("gx", None),
        check_vma=False,
    )
```

```python
import functools

import jax
import jax.numpy as jnp
from jax import lax
from jax.experimental import pallas as pl
from jax.experimental.pallas import tpu as pltpu
from jax.sharding import PartitionSpec as P

CAP = 2048
PAD_MARK = -1024.0


sharpness = 8.0
alpha_mix = 0.8


def normalize(embeds):
    wide = embeds.astype(jnp.float32)
    return (wide * lax.rsqrt(jnp.sum(wide * wide, axis=1, keepdims=True) + 1e-06)).astype(
        jnp.bfloat16
    )


def a2a_kernel(count, *refs):
    x_refs = refs[:count]
    o_refs = refs[count : 2 * count]
    send_sem, recv_sem, local_sem = refs[2 * count :]
    n = x_refs[0].shape[0]
    me = lax.axis_index("gx")
    core = lax.axis_index("ta")
    mesh_ids = pl.DeviceIdType.MESH
    barrier = pltpu.get_barrier_semaphore()

    def greet(i, carry):
        peer = lax.rem(me + 1 + i, n)
        pl.semaphore_signal(barrier, 1, device_id=(peer, core), device_id_type=mesh_ids)
        return carry

    lax.fori_loop(0, n - 1, greet, 0)
    pl.semaphore_wait(barrier, n - 1)
    locals_ = [
        pltpu.make_async_copy(x.at[me], o.at[me], local_sem.at[k])
        for k, (x, o) in enumerate(zip(x_refs, o_refs))
    ]
    for local in locals_:
        local.start()

    def copy_with(k, peer, block_from, block_to):
        return pltpu.make_async_remote_copy(
            x_refs[k].at[block_from],
            o_refs[k].at[block_to],
            send_sem.at[k, block_from],
            recv_sem.at[k, block_to],
            device_id=(peer, core),
            device_id_type=mesh_ids,
        )

    def send(i, carry):
        peer = lax.rem(me + 1 + i, n)
        for k in range(count):
            copy_with(k, peer, peer, me).start()
        return carry

    lax.fori_loop(0, n - 1, send, 0)

    def finish(i, carry):
        peer = lax.rem(me + 1 + i, n)
        for k in range(count):
            copy_with(k, peer, peer, me).wait_send()
            copy_with(k, peer, peer, peer).wait_recv()
        return carry

    lax.fori_loop(0, n - 1, finish, 0)
    for local in locals_:
        local.wait()


def all_to_all(arrays, collective_id):
    count = len(arrays)
    n = arrays[0].shape[0]
    return pl.pallas_call(
        functools.partial(a2a_kernel, count),
        out_shape=[jax.ShapeDtypeStruct(x.shape, x.dtype) for x in arrays],
        in_specs=[pl.BlockSpec(memory_space=pltpu.VMEM)] * count,
        out_specs=[pl.BlockSpec(memory_space=pltpu.VMEM)] * count,
        scratch_shapes=[
            pltpu.SemaphoreType.DMA((count, n)),
            pltpu.SemaphoreType.DMA((count, n)),
            pltpu.SemaphoreType.DMA((count,)),
        ],
        compiler_params=pltpu.CompilerParams(collective_id=collective_id, has_side_effects=True),
    )(*arrays)


def bucket_weights(unit, valid):
    cap = unit.shape[0]
    block = cap
    cols = jnp.arange(cap)
    blocks = []
    dens = []
    for start in range(0, cap, block):
        gram = lax.dot_general(
            unit[start : start + block],
            unit,
            (((1,), (1,)), ((), ())),
            preferred_element_type=jnp.float32,
        )
        keep = valid[None, :] * (cols[None, :] != (start + jnp.arange(block))[:, None]).astype(
            jnp.float32
        )
        weights = (jnp.exp(sharpness * gram) * keep).astype(jnp.bfloat16)
        blocks.append(weights)
        dens.append(jnp.sum(weights.astype(jnp.float32), axis=1))
    return blocks, jnp.concatenate(dens, axis=0)


def weighted_sums(blocks, feats):
    return jnp.concatenate(
        [jnp.dot(w, feats, preferred_element_type=jnp.float32) for w in blocks], axis=0
    )


def body(embeddings, labels, bucket_ids):
    groups = lax.axis_size("gx")
    rows = embeddings.shape[0]
    slot = CAP // groups
    width_l = labels.shape[1]
    ids = bucket_ids[0, :, 0]
    pos = jnp.arange(rows, dtype=jnp.int32)
    same = (ids[:, None] == ids[None, :]) & (pos[None, :] < pos[:, None])
    rank = jnp.sum(same.astype(jnp.int32), axis=1)
    target = ids * slot + rank
    slots = jnp.arange(groups * slot, dtype=jnp.int32)
    place_mat = (target[None, :] == slots[:, None]).astype(jnp.bfloat16)
    occupied = jnp.sum(place_mat.astype(jnp.float32), axis=1) > 0.5
    prior = labels.astype(jnp.float32)

    def place(payload):
        return jnp.dot(place_mat, payload, preferred_element_type=jnp.float32).astype(payload.dtype)

    def exchange(buffer):
        return lax.all_to_all(buffer, "gx", split_axis=0, concat_axis=0, tiled=True)

    def other_core(values):
        return lax.ppermute(values, "ta", perm=[(0, 1), (1, 0)])

    unit_here = normalize(embeddings)
    placed = place(jnp.concatenate([unit_here, labels], axis=1))
    column = lax.broadcasted_iota(jnp.int32, placed.shape, 1)
    pad_here = (column == unit_here.shape[1]) & ~occupied[:, None]
    placed = jnp.where(pad_here, jnp.bfloat16(PAD_MARK), placed)
    got = exchange(placed.reshape(groups, slot, -1)).reshape(groups * slot, -1)
    unit = got[:, : unit_here.shape[1]]
    feats0 = got[:, unit_here.shape[1] :]
    valid = (feats0[:, 0].astype(jnp.float32) > PAD_MARK * 0.5).astype(jnp.float32)

    blocks, den = bucket_weights(unit, valid)
    num1 = weighted_sums(blocks, feats0)

    back_num, back_den = all_to_all([num1.reshape(groups, slot, width_l), den.reshape(groups, slot)], 0)
    back_num = back_num.reshape(groups * slot, width_l)
    back_den = back_den.reshape(groups * slot)
    row_num = back_num[target]
    row_den = jnp.sum(jnp.where(target[None, :] == slots[:, None], back_den[:, None], 0.0), axis=0)
    other_num, other_den = other_core((row_num, row_den))
    total_num = row_num + other_num
    total_den = row_den + other_den
    scale = (1.0 + total_den)[:, None]
    first = (1.0 - alpha_mix) * prior + alpha_mix * total_num / scale

    feats1 = exchange(place(first.astype(jnp.bfloat16)).reshape(groups, slot, -1))
    num2 = weighted_sums(blocks, feats1.reshape(groups * slot, -1))
    back2 = exchange(num2.reshape(groups, slot, -1)).reshape(groups * slot, -1)
    halves = []
    for part in range(2):
        rows_part = slice(part * (rows // 2), (part + 1) * (rows // 2))
        row_num2 = back2[target[rows_part]]
        total_num2 = row_num2 + other_core(row_num2)
        halves.append(
            (1.0 - alpha_mix) * prior[rows_part] + alpha_mix * total_num2 / scale[rows_part]
        )
    return jnp.concatenate(halves, axis=0)


def solution(mesh):
    return jax.shard_map(
        body,
        mesh=mesh,
        in_specs=(P("gx", None), P("gx", None), P("ta", "gx", None)),
        out_specs=P("gx", None),
        check_vma=False,
    )
```

```python
import functools

import jax
import jax.numpy as jnp
from jax import lax
from jax.experimental import pallas as pl
from jax.experimental.pallas import tpu as pltpu
from jax.sharding import PartitionSpec as P

CAP = 2048
PAD_MARK = -1024.0


sharpness = 8.0
alpha_mix = 0.8


def normalize(embeds):
    wide = embeds.astype(jnp.float32)
    return (wide * lax.rsqrt(jnp.sum(wide * wide, axis=1, keepdims=True) + 1e-06)).astype(
        jnp.bfloat16
    )


def a2a_kernel(count, *refs):
    x_refs = refs[:count]
    o_refs = refs[count : 2 * count]
    send_sem, recv_sem, local_sem = refs[2 * count :]
    n = x_refs[0].shape[0]
    me = lax.axis_index("gx")
    core = lax.axis_index("ta")
    mesh_ids = pl.DeviceIdType.MESH
    barrier = pltpu.get_barrier_semaphore()

    def greet(i, carry):
        peer = lax.rem(me + 1 + i, n)
        pl.semaphore_signal(barrier, 1, device_id=(peer, core), device_id_type=mesh_ids)
        return carry

    lax.fori_loop(0, n - 1, greet, 0)
    pl.semaphore_wait(barrier, n - 1)
    locals_ = [
        pltpu.make_async_copy(x.at[me], o.at[me], local_sem.at[k])
        for k, (x, o) in enumerate(zip(x_refs, o_refs))
    ]
    for local in locals_:
        local.start()

    def copy_with(k, peer, block_from, block_to):
        return pltpu.make_async_remote_copy(
            x_refs[k].at[block_from],
            o_refs[k].at[block_to],
            send_sem.at[k, block_from],
            recv_sem.at[k, block_to],
            device_id=(peer, core),
            device_id_type=mesh_ids,
        )

    def send(i, carry):
        peer = lax.rem(me + 1 + i, n)
        for k in range(count):
            copy_with(k, peer, peer, me).start()
        return carry

    lax.fori_loop(0, n - 1, send, 0)

    def finish(i, carry):
        peer = lax.rem(me + 1 + i, n)
        for k in range(count):
            copy_with(k, peer, peer, me).wait_send()
            copy_with(k, peer, peer, peer).wait_recv()
        return carry

    lax.fori_loop(0, n - 1, finish, 0)
    for local in locals_:
        local.wait()


def all_to_all(arrays, collective_id):
    count = len(arrays)
    n = arrays[0].shape[0]
    return pl.pallas_call(
        functools.partial(a2a_kernel, count),
        out_shape=[jax.ShapeDtypeStruct(x.shape, x.dtype) for x in arrays],
        in_specs=[pl.BlockSpec(memory_space=pl.ANY)] * count,
        out_specs=[pl.BlockSpec(memory_space=pl.ANY)] * count,
        scratch_shapes=[
            pltpu.SemaphoreType.DMA((count, n)),
            pltpu.SemaphoreType.DMA((count, n)),
            pltpu.SemaphoreType.DMA((count,)),
        ],
        compiler_params=pltpu.CompilerParams(collective_id=collective_id, has_side_effects=True),
    )(*arrays)


def bucket_weights(unit, valid):
    cap = unit.shape[0]
    block = cap
    cols = jnp.arange(cap)
    blocks = []
    dens = []
    for start in range(0, cap, block):
        gram = lax.dot_general(
            unit[start : start + block],
            unit,
            (((1,), (1,)), ((), ())),
            preferred_element_type=jnp.float32,
        )
        keep = valid[None, :] * (cols[None, :] != (start + jnp.arange(block))[:, None]).astype(
            jnp.float32
        )
        weights = (jnp.exp(sharpness * gram) * keep).astype(jnp.bfloat16)
        blocks.append(weights)
        dens.append(jnp.sum(weights.astype(jnp.float32), axis=1))
    return blocks, jnp.concatenate(dens, axis=0)


def weighted_sums(blocks, feats):
    return jnp.concatenate(
        [jnp.dot(w, feats, preferred_element_type=jnp.float32) for w in blocks], axis=0
    )


def body(embeddings, labels, bucket_ids):
    groups = lax.axis_size("gx")
    rows = embeddings.shape[0]
    slot = CAP // groups
    width_l = labels.shape[1]
    ids = bucket_ids[0, :, 0]
    pos = jnp.arange(rows, dtype=jnp.int32)
    same = (ids[:, None] == ids[None, :]) & (pos[None, :] < pos[:, None])
    rank = jnp.sum(same.astype(jnp.int32), axis=1)
    target = ids * slot + rank
    slots = jnp.arange(groups * slot, dtype=jnp.int32)
    place_mat = (target[None, :] == slots[:, None]).astype(jnp.bfloat16)
    occupied = jnp.sum(place_mat.astype(jnp.float32), axis=1) > 0.5
    prior = labels.astype(jnp.float32)

    def place(payload):
        return jnp.dot(place_mat, payload, preferred_element_type=jnp.float32).astype(payload.dtype)

    def to_items(values):
        hi = values.astype(jnp.bfloat16)
        lo = (values - hi.astype(jnp.float32)).astype(jnp.bfloat16)
        pick = lambda part: lax.dot_general(
            place_mat, part, (((0,), (0,)), ((), ())), preferred_element_type=jnp.float32
        )
        return pick(hi) + pick(lo)

    def exchange(buffer):
        return lax.all_to_all(buffer, "gx", split_axis=0, concat_axis=0, tiled=True)

    def other_core(values):
        return lax.ppermute(values, "ta", perm=[(0, 1), (1, 0)])

    unit_here = normalize(embeddings)
    placed = place(jnp.concatenate([unit_here, labels], axis=1))
    column = lax.broadcasted_iota(jnp.int32, placed.shape, 1)
    pad_here = (column == unit_here.shape[1]) & ~occupied[:, None]
    placed = jnp.where(pad_here, jnp.bfloat16(PAD_MARK), placed)
    got = exchange(placed.reshape(groups, slot, -1)).reshape(groups * slot, -1)
    unit = got[:, : unit_here.shape[1]]
    feats0 = got[:, unit_here.shape[1] :]
    valid = (feats0[:, 0].astype(jnp.float32) > PAD_MARK * 0.5).astype(jnp.float32)

    blocks, den = bucket_weights(unit, valid)
    num1 = weighted_sums(blocks, feats0)

    back_num, back_den = all_to_all([num1.reshape(groups, slot, width_l), den.reshape(groups, slot)], 0)
    back_num = back_num.reshape(groups * slot, width_l)
    back_den = back_den.reshape(groups * slot)
    row_num = to_items(back_num)
    row_den = jnp.sum(jnp.where(target[None, :] == slots[:, None], back_den[:, None], 0.0), axis=0)
    other_num, other_den = other_core((row_num, row_den))
    total_num = row_num + other_num
    total_den = row_den + other_den
    scale = (1.0 + total_den)[:, None]
    first = (1.0 - alpha_mix) * prior + alpha_mix * total_num / scale

    feats1 = exchange(place(first.astype(jnp.bfloat16)).reshape(groups, slot, -1))
    num2 = weighted_sums(blocks, feats1.reshape(groups * slot, -1))
    back2 = exchange(num2.reshape(groups, slot, -1)).reshape(groups * slot, -1)
    row_num2 = to_items(back2)
    total_num2 = row_num2 + other_core(row_num2)
    return (1.0 - alpha_mix) * prior + alpha_mix * total_num2 / scale


def solution(mesh):
    return jax.shard_map(
        body,
        mesh=mesh,
        in_specs=(P("gx", None), P("gx", None), P("ta", "gx", None)),
        out_specs=P("gx", None),
        check_vma=False,
    )
```

```python
import functools

import jax
import jax.numpy as jnp
from jax import lax
from jax.experimental import pallas as pl
from jax.experimental.pallas import tpu as pltpu
from jax.sharding import PartitionSpec as P

CAP = 2048
PAD_MARK = -1024.0


sharpness = 8.0
alpha_mix = 0.8


def normalize(embeds):
    wide = embeds.astype(jnp.float32)
    return (wide * lax.rsqrt(jnp.sum(wide * wide, axis=1, keepdims=True) + 1e-06)).astype(
        jnp.bfloat16
    )


def a2a_kernel(count, *refs):
    x_refs = refs[:count]
    o_refs = refs[count : 2 * count]
    send_sem, recv_sem, local_sem = refs[2 * count :]
    n = x_refs[0].shape[0]
    me = lax.axis_index("gx")
    core = lax.axis_index("ta")
    mesh_ids = pl.DeviceIdType.MESH
    barrier = pltpu.get_barrier_semaphore()

    def greet(i, carry):
        peer = lax.rem(me + 1 + i, n)
        pl.semaphore_signal(barrier, 1, device_id=(peer, core), device_id_type=mesh_ids)
        return carry

    lax.fori_loop(0, n - 1, greet, 0)
    pl.semaphore_wait(barrier, n - 1)
    locals_ = [
        pltpu.make_async_copy(x.at[me], o.at[me], local_sem.at[k])
        for k, (x, o) in enumerate(zip(x_refs, o_refs))
    ]
    for local in locals_:
        local.start()

    def copy_with(k, peer, block_from, block_to):
        return pltpu.make_async_remote_copy(
            x_refs[k].at[block_from],
            o_refs[k].at[block_to],
            send_sem.at[k, block_from],
            recv_sem.at[k, block_to],
            device_id=(peer, core),
            device_id_type=mesh_ids,
        )

    def send(i, carry):
        peer = lax.rem(me + 1 + i, n)
        for k in range(count):
            copy_with(k, peer, peer, me).start()
        return carry

    lax.fori_loop(0, n - 1, send, 0)

    def finish(i, carry):
        peer = lax.rem(me + 1 + i, n)
        for k in range(count):
            copy_with(k, peer, peer, me).wait_send()
            copy_with(k, peer, peer, peer).wait_recv()
        return carry

    lax.fori_loop(0, n - 1, finish, 0)
    for local in locals_:
        local.wait()


def all_to_all(arrays, collective_id):
    count = len(arrays)
    n = arrays[0].shape[0]
    return pl.pallas_call(
        functools.partial(a2a_kernel, count),
        out_shape=[jax.ShapeDtypeStruct(x.shape, x.dtype) for x in arrays],
        in_specs=[pl.BlockSpec(memory_space=pl.ANY)] * count,
        out_specs=[pl.BlockSpec(memory_space=pl.ANY)] * count,
        scratch_shapes=[
            pltpu.SemaphoreType.DMA((count, n)),
            pltpu.SemaphoreType.DMA((count, n)),
            pltpu.SemaphoreType.DMA((count,)),
        ],
        compiler_params=pltpu.CompilerParams(collective_id=collective_id, has_side_effects=True),
    )(*arrays)


def bucket_weights(unit, valid):
    cap = unit.shape[0]
    block = cap
    cols = jnp.arange(cap)
    blocks = []
    dens = []
    for start in range(0, cap, block):
        gram = lax.dot_general(
            unit[start : start + block],
            unit,
            (((1,), (1,)), ((), ())),
            preferred_element_type=jnp.float32,
        )
        keep = valid[None, :] * (cols[None, :] != (start + jnp.arange(block))[:, None]).astype(
            jnp.float32
        )
        weights = (jnp.exp(sharpness * gram) * keep).astype(jnp.bfloat16)
        blocks.append(weights)
        dens.append(jnp.sum(weights.astype(jnp.float32), axis=1))
    return blocks, jnp.concatenate(dens, axis=0)


def weighted_sums(blocks, feats):
    return jnp.concatenate(
        [jnp.dot(w, feats, preferred_element_type=jnp.float32) for w in blocks], axis=0
    )


def body(embeddings, labels, bucket_ids):
    groups = lax.axis_size("gx")
    rows = embeddings.shape[0]
    slot = CAP // groups
    width_l = labels.shape[1]
    ids = bucket_ids[0, :, 0]
    pos = jnp.arange(rows, dtype=jnp.int32)
    same = (ids[:, None] == ids[None, :]) & (pos[None, :] < pos[:, None])
    rank = jnp.sum(same.astype(jnp.int32), axis=1)
    target = ids * slot + rank
    slots = jnp.arange(groups * slot, dtype=jnp.int32)
    place_mat = (target[None, :] == slots[:, None]).astype(jnp.bfloat16)
    occupied = jnp.sum(place_mat.astype(jnp.float32), axis=1) > 0.5
    prior = labels.astype(jnp.float32)

    def place(payload):
        return jnp.dot(place_mat, payload, preferred_element_type=jnp.float32).astype(payload.dtype)

    def to_items(values):
        hi = lax.reduce_precision(values, exponent_bits=8, mantissa_bits=7)
        lo = values - hi
        pick = lambda part: lax.dot_general(
            place_mat,
            part.astype(jnp.bfloat16),
            (((0,), (0,)), ((), ())),
            preferred_element_type=jnp.float32,
        )
        return pick(hi) + pick(lo)

    def exchange(buffer):
        return lax.all_to_all(buffer, "gx", split_axis=0, concat_axis=0, tiled=True)

    def other_core(values):
        return lax.ppermute(values, "ta", perm=[(0, 1), (1, 0)])

    unit_here = normalize(embeddings)
    placed = place(jnp.concatenate([unit_here, labels], axis=1))
    column = lax.broadcasted_iota(jnp.int32, placed.shape, 1)
    pad_here = (column == unit_here.shape[1]) & ~occupied[:, None]
    placed = jnp.where(pad_here, jnp.bfloat16(PAD_MARK), placed)
    got = exchange(placed.reshape(groups, slot, -1)).reshape(groups * slot, -1)
    unit = got[:, : unit_here.shape[1]]
    feats0 = got[:, unit_here.shape[1] :]
    valid = (feats0[:, 0].astype(jnp.float32) > PAD_MARK * 0.5).astype(jnp.float32)

    blocks, den = bucket_weights(unit, valid)
    num1 = weighted_sums(blocks, feats0)

    back_num, back_den = all_to_all([num1.reshape(groups, slot, width_l), den.reshape(groups, slot)], 0)
    back_num = back_num.reshape(groups * slot, width_l)
    back_den = back_den.reshape(groups * slot)
    row_num = to_items(back_num)
    row_den = jnp.sum(jnp.where(target[None, :] == slots[:, None], back_den[:, None], 0.0), axis=0)
    other_num, other_den = other_core((row_num, row_den))
    total_num = row_num + other_num
    total_den = row_den + other_den
    scale = (1.0 + total_den)[:, None]
    first = (1.0 - alpha_mix) * prior + alpha_mix * total_num / scale

    feats1 = exchange(place(first.astype(jnp.bfloat16)).reshape(groups, slot, -1))
    num2 = weighted_sums(blocks, feats1.reshape(groups * slot, -1))
    back2 = exchange(num2.reshape(groups, slot, -1)).reshape(groups * slot, -1)
    row_num2 = to_items(back2)
    total_num2 = row_num2 + other_core(row_num2)
    return (1.0 - alpha_mix) * prior + alpha_mix * total_num2 / scale


def solution(mesh):
    return jax.shard_map(
        body,
        mesh=mesh,
        in_specs=(P("gx", None), P("gx", None), P("ta", "gx", None)),
        out_specs=P("gx", None),
        check_vma=False,
    )
```

```python
import functools

import jax
import jax.numpy as jnp
from jax import lax
from jax.experimental import pallas as pl
from jax.experimental.pallas import tpu as pltpu
from jax.sharding import PartitionSpec as P

CAP = 2048
PAD_MARK = -1024.0


sharpness = 8.0
alpha_mix = 0.8


def normalize(embeds):
    wide = embeds.astype(jnp.float32)
    return (wide * lax.rsqrt(jnp.sum(wide * wide, axis=1, keepdims=True) + 1e-06)).astype(
        jnp.bfloat16
    )


def a2a_kernel(count, *refs):
    x_refs = refs[:count]
    o_refs = refs[count : 2 * count]
    send_sem, recv_sem, local_sem = refs[2 * count :]
    n = x_refs[0].shape[0]
    me = lax.axis_index("gx")
    core = lax.axis_index("ta")
    mesh_ids = pl.DeviceIdType.MESH
    barrier = pltpu.get_barrier_semaphore()

    def greet(i, carry):
        peer = lax.rem(me + 1 + i, n)
        pl.semaphore_signal(barrier, 1, device_id=(peer, core), device_id_type=mesh_ids)
        return carry

    lax.fori_loop(0, n - 1, greet, 0)
    pl.semaphore_wait(barrier, n - 1)
    locals_ = [
        pltpu.make_async_copy(x.at[me], o.at[me], local_sem.at[k])
        for k, (x, o) in enumerate(zip(x_refs, o_refs))
    ]
    for local in locals_:
        local.start()

    def copy_with(k, peer, block_from, block_to):
        return pltpu.make_async_remote_copy(
            x_refs[k].at[block_from],
            o_refs[k].at[block_to],
            send_sem.at[k, block_from],
            recv_sem.at[k, block_to],
            device_id=(peer, core),
            device_id_type=mesh_ids,
        )

    def partner(i):
        return lax.rem(me + (1 - 2 * lax.rem(i, 2)) * (i // 2 + 1) + n, n)

    def send(i, carry):
        peer = partner(i)
        for k in range(count):
            copy_with(k, peer, peer, me).start()
        return carry

    lax.fori_loop(0, n - 1, send, 0)

    def finish(i, carry):
        peer = partner(i)
        for k in range(count):
            copy_with(k, peer, peer, me).wait_send()
            copy_with(k, peer, peer, peer).wait_recv()
        return carry

    lax.fori_loop(0, n - 1, finish, 0)
    for local in locals_:
        local.wait()


def all_to_all(arrays, collective_id):
    count = len(arrays)
    n = arrays[0].shape[0]
    return pl.pallas_call(
        functools.partial(a2a_kernel, count),
        out_shape=[jax.ShapeDtypeStruct(x.shape, x.dtype) for x in arrays],
        in_specs=[pl.BlockSpec(memory_space=pl.ANY)] * count,
        out_specs=[pl.BlockSpec(memory_space=pl.ANY)] * count,
        scratch_shapes=[
            pltpu.SemaphoreType.DMA((count, n)),
            pltpu.SemaphoreType.DMA((count, n)),
            pltpu.SemaphoreType.DMA((count,)),
        ],
        compiler_params=pltpu.CompilerParams(collective_id=collective_id, has_side_effects=True),
    )(*arrays)


def bucket_weights(unit, valid):
    cap = unit.shape[0]
    block = cap
    cols = jnp.arange(cap)
    blocks = []
    dens = []
    for start in range(0, cap, block):
        gram = lax.dot_general(
            unit[start : start + block],
            unit,
            (((1,), (1,)), ((), ())),
            preferred_element_type=jnp.float32,
        )
        keep = valid[None, :] * (cols[None, :] != (start + jnp.arange(block))[:, None]).astype(
            jnp.float32
        )
        weights = (jnp.exp(sharpness * gram) * keep).astype(jnp.bfloat16)
        blocks.append(weights)
        dens.append(jnp.sum(weights.astype(jnp.float32), axis=1))
    return blocks, jnp.concatenate(dens, axis=0)


def weighted_sums(blocks, feats):
    return jnp.concatenate(
        [jnp.dot(w, feats, preferred_element_type=jnp.float32) for w in blocks], axis=0
    )


def body(embeddings, labels, bucket_ids):
    groups = lax.axis_size("gx")
    rows = embeddings.shape[0]
    slot = CAP // groups
    width_l = labels.shape[1]
    ids = bucket_ids[0, :, 0]
    pos = jnp.arange(rows, dtype=jnp.int32)
    same = (ids[:, None] == ids[None, :]) & (pos[None, :] < pos[:, None])
    rank = jnp.sum(same.astype(jnp.int32), axis=1)
    target = ids * slot + rank
    slots = jnp.arange(groups * slot, dtype=jnp.int32)
    place_mat = (target[None, :] == slots[:, None]).astype(jnp.bfloat16)
    occupied = jnp.sum(place_mat.astype(jnp.float32), axis=1) > 0.5
    prior = labels.astype(jnp.float32)

    def place(payload):
        return jnp.dot(place_mat, payload, preferred_element_type=jnp.float32).astype(payload.dtype)

    def to_items(values):
        hi = lax.reduce_precision(values, exponent_bits=8, mantissa_bits=7)
        lo = values - hi
        pick = lambda part: lax.dot_general(
            place_mat,
            part.astype(jnp.bfloat16),
            (((0,), (0,)), ((), ())),
            preferred_element_type=jnp.float32,
        )
        return pick(hi) + pick(lo)

    def exchange(buffer):
        return lax.all_to_all(buffer, "gx", split_axis=0, concat_axis=0, tiled=True)

    def other_core(values):
        return lax.ppermute(values, "ta", perm=[(0, 1), (1, 0)])

    unit_here = normalize(embeddings)
    placed = place(jnp.concatenate([unit_here, labels], axis=1))
    column = lax.broadcasted_iota(jnp.int32, placed.shape, 1)
    pad_here = (column == unit_here.shape[1]) & ~occupied[:, None]
    placed = jnp.where(pad_here, jnp.bfloat16(PAD_MARK), placed)
    got = exchange(placed.reshape(groups, slot, -1)).reshape(groups * slot, -1)
    unit = got[:, : unit_here.shape[1]]
    feats0 = got[:, unit_here.shape[1] :]
    valid = (feats0[:, 0].astype(jnp.float32) > PAD_MARK * 0.5).astype(jnp.float32)

    blocks, den = bucket_weights(unit, valid)
    num1 = weighted_sums(blocks, feats0)

    back_num, back_den = all_to_all([num1.reshape(groups, slot, width_l), den.reshape(groups, slot)], 0)
    back_num = back_num.reshape(groups * slot, width_l)
    back_den = back_den.reshape(groups * slot)
    row_num = to_items(back_num)
    row_den = jnp.sum(jnp.where(target[None, :] == slots[:, None], back_den[:, None], 0.0), axis=0)
    other_num, other_den = other_core((row_num, row_den))
    total_num = row_num + other_num
    total_den = row_den + other_den
    scale = (1.0 + total_den)[:, None]
    first = (1.0 - alpha_mix) * prior + alpha_mix * total_num / scale

    feats1 = exchange(place(first.astype(jnp.bfloat16)).reshape(groups, slot, -1))
    num2 = weighted_sums(blocks, feats1.reshape(groups * slot, -1))
    back2 = exchange(num2.reshape(groups, slot, -1)).reshape(groups * slot, -1)
    row_num2 = to_items(back2)
    total_num2 = row_num2 + other_core(row_num2)
    return (1.0 - alpha_mix) * prior + alpha_mix * total_num2 / scale


def solution(mesh):
    return jax.shard_map(
        body,
        mesh=mesh,
        in_specs=(P("gx", None), P("gx", None), P("ta", "gx", None)),
        out_specs=P("gx", None),
        check_vma=False,
    )
```

```python
import functools

import jax
import jax.numpy as jnp
from jax import lax
from jax.experimental import pallas as pl
from jax.experimental.pallas import tpu as pltpu
from jax.sharding import PartitionSpec as P

CAP = 2048
PAD_MARK = -1024.0


sharpness = 8.0
alpha_mix = 0.8


def normalize(embeds):
    wide = embeds.astype(jnp.float32)
    return (wide * lax.rsqrt(jnp.sum(wide * wide, axis=1, keepdims=True) + 1e-06)).astype(
        jnp.bfloat16
    )


def a2a_kernel(count, *refs):
    x_refs = refs[:count]
    o_refs = refs[count : 2 * count]
    send_sem, recv_sem, local_sem = refs[2 * count :]
    n = x_refs[0].shape[0]
    me = lax.axis_index("gx")
    core = lax.axis_index("ta")
    mesh_ids = pl.DeviceIdType.MESH
    barrier = pltpu.get_barrier_semaphore()

    def greet(i, carry):
        peer = lax.rem(me + 1 + i, n)
        pl.semaphore_signal(barrier, 1, device_id=(peer, core), device_id_type=mesh_ids)
        return carry

    lax.fori_loop(0, n - 1, greet, 0)
    pl.semaphore_wait(barrier, n - 1)
    locals_ = [
        pltpu.make_async_copy(x.at[me], o.at[me], local_sem.at[k])
        for k, (x, o) in enumerate(zip(x_refs, o_refs))
    ]
    for local in locals_:
        local.start()

    def copy_with(k, peer, block_from, block_to):
        return pltpu.make_async_remote_copy(
            x_refs[k].at[block_from],
            o_refs[k].at[block_to],
            send_sem.at[k, block_from],
            recv_sem.at[k, block_to],
            device_id=(peer, core),
            device_id_type=mesh_ids,
        )

    def partner(i):
        return lax.rem(me + (1 - 2 * lax.rem(i, 2)) * (i // 2 + 1) + n, n)

    def send(i, carry):
        peer = partner(i)
        for k in range(count):
            copy_with(k, peer, peer, me).start()
        return carry

    lax.fori_loop(0, n - 1, send, 0)

    def finish(i, carry):
        peer = partner(i)
        for k in range(count):
            copy_with(k, peer, peer, me).wait_send()
            copy_with(k, peer, peer, peer).wait_recv()
        return carry

    lax.fori_loop(0, n - 1, finish, 0)
    for local in locals_:
        local.wait()


def all_to_all(arrays, collective_id):
    count = len(arrays)
    n = arrays[0].shape[0]
    return pl.pallas_call(
        functools.partial(a2a_kernel, count),
        out_shape=[jax.ShapeDtypeStruct(x.shape, x.dtype) for x in arrays],
        in_specs=[pl.BlockSpec(memory_space=pl.ANY)] * count,
        out_specs=[pl.BlockSpec(memory_space=pl.ANY)] * count,
        scratch_shapes=[
            pltpu.SemaphoreType.DMA((count, n)),
            pltpu.SemaphoreType.DMA((count, n)),
            pltpu.SemaphoreType.DMA((count,)),
        ],
        compiler_params=pltpu.CompilerParams(collective_id=collective_id, has_side_effects=True),
    )(*arrays)


def bucket_weights(unit, valid):
    cap = unit.shape[0]
    block = cap
    cols = jnp.arange(cap)
    blocks = []
    dens = []
    for start in range(0, cap, block):
        gram = lax.dot_general(
            unit[start : start + block],
            unit,
            (((1,), (1,)), ((), ())),
            preferred_element_type=jnp.float32,
        )
        keep = valid[None, :] * (cols[None, :] != (start + jnp.arange(block))[:, None]).astype(
            jnp.float32
        )
        weights = (jnp.exp(sharpness * gram) * keep).astype(jnp.bfloat16)
        blocks.append(weights)
        dens.append(jnp.sum(weights.astype(jnp.float32), axis=1))
    return blocks, jnp.concatenate(dens, axis=0)


def weighted_sums(blocks, feats):
    return jnp.concatenate(
        [jnp.dot(w, feats, preferred_element_type=jnp.float32) for w in blocks], axis=0
    )


def body(embeddings, labels, bucket_ids):
    groups = lax.axis_size("gx")
    rows = embeddings.shape[0]
    slot = CAP // groups
    width_l = labels.shape[1]
    ids = bucket_ids[0, :, 0]
    pos = jnp.arange(rows, dtype=jnp.int32)
    same = (ids[:, None] == ids[None, :]) & (pos[None, :] < pos[:, None])
    rank = jnp.sum(same.astype(jnp.int32), axis=1)
    target = ids * slot + rank
    slots = jnp.arange(groups * slot, dtype=jnp.int32)
    place_mat = (target[None, :] == slots[:, None]).astype(jnp.bfloat16)
    occupied = jnp.sum(place_mat.astype(jnp.float32), axis=1) > 0.5
    prior = labels.astype(jnp.float32)

    def place(payload):
        return jnp.dot(place_mat, payload, preferred_element_type=jnp.float32).astype(payload.dtype)

    def to_items(values):
        hi = lax.reduce_precision(values, exponent_bits=8, mantissa_bits=7)
        lo = values - hi
        pick = lambda part: lax.dot_general(
            place_mat,
            part.astype(jnp.bfloat16),
            (((0,), (0,)), ((), ())),
            preferred_element_type=jnp.float32,
        )
        return pick(hi) + pick(lo)

    def exchange(buffer):
        return lax.all_to_all(buffer, "gx", split_axis=0, concat_axis=0, tiled=True)

    def other_core(values):
        return lax.ppermute(values, "ta", perm=[(0, 1), (1, 0)])

    unit_here = normalize(embeddings)
    placed = place(jnp.concatenate([unit_here, labels], axis=1))
    column = lax.broadcasted_iota(jnp.int32, placed.shape, 1)
    pad_here = (column == unit_here.shape[1]) & ~occupied[:, None]
    placed = jnp.where(pad_here, jnp.bfloat16(PAD_MARK), placed)
    got = exchange(placed.reshape(groups, slot, -1)).reshape(groups * slot, -1)
    unit = got[:, : unit_here.shape[1]]
    feats0 = got[:, unit_here.shape[1] :]
    valid = (feats0[:, 0].astype(jnp.float32) > PAD_MARK * 0.5).astype(jnp.float32)

    blocks, den = bucket_weights(unit, valid)
    num1 = weighted_sums(blocks, feats0)

    back_num, back_den = all_to_all([num1.reshape(groups, slot, width_l), den.reshape(groups, slot)], 0)
    back_num = back_num.reshape(groups * slot, width_l)
    back_den = back_den.reshape(groups * slot)
    row_num = to_items(back_num)
    row_den = jnp.sum(jnp.where(target[None, :] == slots[:, None], back_den[:, None], 0.0), axis=0)
    other_num, other_den = other_core((row_num, row_den))
    total_num = row_num + other_num
    total_den = row_den + other_den
    scale = (1.0 + total_den)[:, None]
    first = (1.0 - alpha_mix) * prior + alpha_mix * total_num / scale

    feats1 = exchange(place(first.astype(jnp.bfloat16)).reshape(groups, slot, -1))
    num2 = weighted_sums(blocks, feats1.reshape(groups * slot, -1))
    (back2,) = all_to_all([num2.reshape(groups, slot, width_l)], 1)
    back2 = back2.reshape(groups * slot, width_l)
    row_num2 = to_items(back2)
    total_num2 = row_num2 + other_core(row_num2)
    return (1.0 - alpha_mix) * prior + alpha_mix * total_num2 / scale


def solution(mesh):
    return jax.shard_map(
        body,
        mesh=mesh,
        in_specs=(P("gx", None), P("gx", None), P("ta", "gx", None)),
        out_specs=P("gx", None),
        check_vma=False,
    )
```

```python
import functools

import jax
import jax.numpy as jnp
from jax import lax
from jax.experimental import pallas as pl
from jax.experimental.pallas import tpu as pltpu
from jax.sharding import PartitionSpec as P

CAP = 2048
PAD_MARK = -1024.0


sharpness = 8.0
alpha_mix = 0.8


def normalize(embeds):
    wide = embeds.astype(jnp.float32)
    return (wide * lax.rsqrt(jnp.sum(wide * wide, axis=1, keepdims=True) + 1e-06)).astype(
        jnp.bfloat16
    )


def a2a_kernel(count, *refs):
    x_refs = refs[:count]
    o_refs = refs[count : 2 * count]
    send_sem, recv_sem, local_sem = refs[2 * count :]
    n = x_refs[0].shape[0]
    me = lax.axis_index("gx")
    core = lax.axis_index("ta")
    mesh_ids = pl.DeviceIdType.MESH
    barrier = pltpu.get_barrier_semaphore()

    def greet(i, carry):
        peer = lax.rem(me + 1 + i, n)
        pl.semaphore_signal(barrier, 1, device_id=(peer, core), device_id_type=mesh_ids)
        return carry

    lax.fori_loop(0, n - 1, greet, 0)
    pl.semaphore_wait(barrier, n - 1)
    locals_ = [
        pltpu.make_async_copy(x.at[me], o.at[me], local_sem.at[k])
        for k, (x, o) in enumerate(zip(x_refs, o_refs))
    ]
    for local in locals_:
        local.start()

    def copy_with(k, peer, block_from, block_to):
        return pltpu.make_async_remote_copy(
            x_refs[k].at[block_from],
            o_refs[k].at[block_to],
            send_sem.at[k, block_from],
            recv_sem.at[k, block_to],
            device_id=(peer, core),
            device_id_type=mesh_ids,
        )

    def partner(i):
        return lax.rem(me + (1 - 2 * lax.rem(i, 2)) * (i // 2 + 1) + n, n)

    def send(i, carry):
        peer = partner(i)
        for k in range(count):
            copy_with(k, peer, peer, me).start()
        return carry

    lax.fori_loop(0, n - 1, send, 0)

    def finish(i, carry):
        peer = partner(i)
        for k in range(count):
            copy_with(k, peer, peer, me).wait_send()
            copy_with(k, peer, peer, peer).wait_recv()
        return carry

    lax.fori_loop(0, n - 1, finish, 0)
    for local in locals_:
        local.wait()


def all_to_all(arrays, collective_id):
    count = len(arrays)
    n = arrays[0].shape[0]
    return pl.pallas_call(
        functools.partial(a2a_kernel, count),
        out_shape=[jax.ShapeDtypeStruct(x.shape, x.dtype) for x in arrays],
        in_specs=[pl.BlockSpec(memory_space=pl.ANY)] * count,
        out_specs=[pl.BlockSpec(memory_space=pl.ANY)] * count,
        scratch_shapes=[
            pltpu.SemaphoreType.DMA((count, n)),
            pltpu.SemaphoreType.DMA((count, n)),
            pltpu.SemaphoreType.DMA((count,)),
        ],
        compiler_params=pltpu.CompilerParams(collective_id=collective_id, has_side_effects=True),
    )(*arrays)


def bucket_weights(unit, valid):
    cap = unit.shape[0]
    block = cap
    cols = jnp.arange(cap)
    blocks = []
    dens = []
    for start in range(0, cap, block):
        gram = lax.dot_general(
            unit[start : start + block],
            unit,
            (((1,), (1,)), ((), ())),
            preferred_element_type=jnp.float32,
        )
        keep = valid[None, :] * (cols[None, :] != (start + jnp.arange(block))[:, None]).astype(
            jnp.float32
        )
        weights = (jnp.exp(sharpness * gram) * keep).astype(jnp.bfloat16)
        blocks.append(weights)
        dens.append(jnp.sum(weights.astype(jnp.float32), axis=1))
    return blocks, jnp.concatenate(dens, axis=0)


def weighted_sums(blocks, feats):
    return jnp.concatenate(
        [jnp.dot(w, feats, preferred_element_type=jnp.float32) for w in blocks], axis=0
    )


def body(embeddings, labels, bucket_ids):
    groups = lax.axis_size("gx")
    rows = embeddings.shape[0]
    slot = CAP // groups
    width_l = labels.shape[1]
    ids = bucket_ids[0, :, 0]
    pos = jnp.arange(rows, dtype=jnp.int32)
    same = (ids[:, None] == ids[None, :]) & (pos[None, :] < pos[:, None])
    rank = jnp.sum(same.astype(jnp.int32), axis=1)
    target = ids * slot + rank
    slots = jnp.arange(groups * slot, dtype=jnp.int32)
    place_mat = (target[None, :] == slots[:, None]).astype(jnp.bfloat16)
    occupied = jnp.sum(place_mat.astype(jnp.float32), axis=1) > 0.5
    prior = labels.astype(jnp.float32)

    def place(payload):
        return jnp.dot(place_mat, payload, preferred_element_type=jnp.float32).astype(payload.dtype)

    def exchange(buffer):
        return lax.all_to_all(buffer, "gx", split_axis=0, concat_axis=0, tiled=True)

    def other_core(values):
        return lax.ppermute(values, "ta", perm=[(0, 1), (1, 0)])

    unit_here = normalize(embeddings)
    placed = place(jnp.concatenate([unit_here, labels], axis=1))
    column = lax.broadcasted_iota(jnp.int32, placed.shape, 1)
    pad_here = (column == unit_here.shape[1]) & ~occupied[:, None]
    placed = jnp.where(pad_here, jnp.bfloat16(PAD_MARK), placed)
    got = exchange(placed.reshape(groups, slot, -1)).reshape(groups * slot, -1)
    unit = got[:, : unit_here.shape[1]]
    feats0 = got[:, unit_here.shape[1] :]
    valid = (feats0[:, 0].astype(jnp.float32) > PAD_MARK * 0.5).astype(jnp.float32)

    blocks, den = bucket_weights(unit, valid)
    num1 = weighted_sums(blocks, feats0)

    back_num, back_den = all_to_all([num1.reshape(groups, slot, width_l), den.reshape(groups, slot)], 0)
    back_num = back_num.reshape(groups * slot, width_l)
    back_den = back_den.reshape(groups * slot)
    row_num = back_num[target]
    row_den = jnp.sum(jnp.where(target[None, :] == slots[:, None], back_den[:, None], 0.0), axis=0)
    other_num, other_den = other_core((row_num, row_den))
    total_num = row_num + other_num
    total_den = row_den + other_den
    scale = (1.0 + total_den)[:, None]
    first = (1.0 - alpha_mix) * prior + alpha_mix * total_num / scale

    feats1 = exchange(place(first.astype(jnp.bfloat16)).reshape(groups, slot, -1))
    num2 = weighted_sums(blocks, feats1.reshape(groups * slot, -1))
    back2 = exchange(num2.reshape(groups, slot, -1)).reshape(groups * slot, -1)
    halves = []
    for part in range(2):
        rows_part = slice(part * (rows // 2), (part + 1) * (rows // 2))
        row_num2 = back2[target[rows_part]]
        total_num2 = row_num2 + other_core(row_num2)
        halves.append(
            (1.0 - alpha_mix) * prior[rows_part] + alpha_mix * total_num2 / scale[rows_part]
        )
    return jnp.concatenate(halves, axis=0)


def solution(mesh):
    return jax.shard_map(
        body,
        mesh=mesh,
        in_specs=(P("gx", None), P("gx", None), P("ta", "gx", None)),
        out_specs=P("gx", None),
        check_vma=False,
    )
```

```python
import functools

import jax
import jax.numpy as jnp
from jax import lax
from jax.experimental import pallas as pl
from jax.experimental.pallas import tpu as pltpu
from jax.sharding import PartitionSpec as P

CAP = 2048
PAD_MARK = -1024.0


sharpness = 8.0
alpha_mix = 0.8


def normalize(embeds):
    wide = embeds.astype(jnp.float32)
    return (wide * lax.rsqrt(jnp.sum(wide * wide, axis=1, keepdims=True) + 1e-06)).astype(
        jnp.bfloat16
    )


def a2a_kernel(count, *refs):
    x_refs = refs[:count]
    o_refs = refs[count : 2 * count]
    send_sem, recv_sem, local_sem = refs[2 * count :]
    n = x_refs[0].shape[0]
    me = lax.axis_index("gx")
    core = lax.axis_index("ta")
    mesh_ids = pl.DeviceIdType.MESH
    barrier = pltpu.get_barrier_semaphore()

    def greet(i, carry):
        peer = lax.rem(me + 1 + i, n)
        pl.semaphore_signal(barrier, 1, device_id=(peer, core), device_id_type=mesh_ids)
        return carry

    lax.fori_loop(0, n - 1, greet, 0)
    pl.semaphore_wait(barrier, n - 1)
    locals_ = [
        pltpu.make_async_copy(x.at[me], o.at[me], local_sem.at[k])
        for k, (x, o) in enumerate(zip(x_refs, o_refs))
    ]
    for local in locals_:
        local.start()

    def copy_with(k, peer, block_from, block_to):
        return pltpu.make_async_remote_copy(
            x_refs[k].at[block_from],
            o_refs[k].at[block_to],
            send_sem.at[k, block_from],
            recv_sem.at[k, block_to],
            device_id=(peer, core),
            device_id_type=mesh_ids,
        )

    def partner(i):
        return lax.rem(me + (1 - 2 * lax.rem(i, 2)) * (i // 2 + 1) + n, n)

    def send(i, carry):
        peer = partner(i)
        for k in range(count):
            copy_with(k, peer, peer, me).start()
        return carry

    lax.fori_loop(0, n - 1, send, 0)

    def finish(i, carry):
        peer = partner(i)
        for k in range(count):
            copy_with(k, peer, peer, me).wait_send()
            copy_with(k, peer, peer, peer).wait_recv()
        return carry

    lax.fori_loop(0, n - 1, finish, 0)
    for local in locals_:
        local.wait()


def all_to_all(arrays, collective_id):
    count = len(arrays)
    n = arrays[0].shape[0]
    return pl.pallas_call(
        functools.partial(a2a_kernel, count),
        out_shape=[jax.ShapeDtypeStruct(x.shape, x.dtype) for x in arrays],
        in_specs=[pl.BlockSpec(memory_space=pl.ANY)] * count,
        out_specs=[pl.BlockSpec(memory_space=pl.ANY)] * count,
        scratch_shapes=[
            pltpu.SemaphoreType.DMA((count, n)),
            pltpu.SemaphoreType.DMA((count, n)),
            pltpu.SemaphoreType.DMA((count,)),
        ],
        compiler_params=pltpu.CompilerParams(collective_id=collective_id, has_side_effects=True),
    )(*arrays)


def bucket_weights(unit, valid):
    cap = unit.shape[0]
    block = cap
    cols = jnp.arange(cap)
    blocks = []
    dens = []
    for start in range(0, cap, block):
        gram = lax.dot_general(
            unit[start : start + block],
            unit,
            (((1,), (1,)), ((), ())),
            preferred_element_type=jnp.float32,
        )
        keep = valid[None, :] * (cols[None, :] != (start + jnp.arange(block))[:, None]).astype(
            jnp.float32
        )
        weights = (jnp.exp(sharpness * gram) * keep).astype(jnp.bfloat16)
        blocks.append(weights)
        dens.append(jnp.sum(weights.astype(jnp.float32), axis=1))
    return blocks, jnp.concatenate(dens, axis=0)


def weighted_sums(blocks, feats):
    return jnp.concatenate(
        [jnp.dot(w, feats, preferred_element_type=jnp.float32) for w in blocks], axis=0
    )


def body(embeddings, labels, bucket_ids):
    groups = lax.axis_size("gx")
    rows = embeddings.shape[0]
    slot = CAP // groups
    width_l = labels.shape[1]
    ids = bucket_ids[0, :, 0]
    pos = jnp.arange(rows, dtype=jnp.int32)
    same = (ids[:, None] == ids[None, :]) & (pos[None, :] < pos[:, None])
    rank = jnp.sum(same.astype(jnp.int32), axis=1)
    target = ids * slot + rank
    slots = jnp.arange(groups * slot, dtype=jnp.int32)
    place_mat = (target[None, :] == slots[:, None]).astype(jnp.bfloat16)
    occupied = jnp.sum(place_mat.astype(jnp.float32), axis=1) > 0.5
    prior = labels.astype(jnp.float32)

    def place(payload):
        return jnp.dot(place_mat, payload, preferred_element_type=jnp.float32).astype(payload.dtype)

    def to_items(values):
        hi = lax.reduce_precision(values, exponent_bits=8, mantissa_bits=7)
        lo = values - hi
        pick = lambda part: lax.dot_general(
            place_mat,
            part.astype(jnp.bfloat16),
            (((0,), (0,)), ((), ())),
            preferred_element_type=jnp.float32,
        )
        return pick(hi) + pick(lo)

    def exchange(buffer):
        return lax.all_to_all(buffer, "gx", split_axis=0, concat_axis=0, tiled=True)

    def other_core(values):
        return lax.ppermute(values, "ta", perm=[(0, 1), (1, 0)])

    unit_here = normalize(embeddings)
    placed = place(jnp.concatenate([unit_here, labels], axis=1))
    column = lax.broadcasted_iota(jnp.int32, placed.shape, 1)
    pad_here = (column == unit_here.shape[1]) & ~occupied[:, None]
    placed = jnp.where(pad_here, jnp.bfloat16(PAD_MARK), placed)
    got = exchange(placed.reshape(groups, slot, -1)).reshape(groups * slot, -1)
    unit = got[:, : unit_here.shape[1]]
    feats0 = got[:, unit_here.shape[1] :]
    valid = (feats0[:, 0].astype(jnp.float32) > PAD_MARK * 0.5).astype(jnp.float32)

    blocks, den = bucket_weights(unit, valid)
    num1 = weighted_sums(blocks, feats0)

    back_num, back_den = all_to_all([num1.reshape(groups, slot, width_l), den.reshape(groups, slot)], 0)
    back_num = back_num.reshape(groups * slot, width_l)
    back_den = back_den.reshape(groups * slot)
    row_num = to_items(back_num)
    row_den = jnp.sum(jnp.where(target[None, :] == slots[:, None], back_den[:, None], 0.0), axis=0)
    other_num, other_den = other_core((row_num, row_den))
    total_num = row_num + other_num
    total_den = row_den + other_den
    scale = (1.0 + total_den)[:, None]
    first = (1.0 - alpha_mix) * prior + alpha_mix * total_num / scale

    (feats1,) = all_to_all([place(first.astype(jnp.bfloat16)).reshape(groups, slot, -1)], 1)
    num2 = weighted_sums(blocks, feats1.reshape(groups * slot, -1))
    back2 = exchange(num2.reshape(groups, slot, -1)).reshape(groups * slot, -1)
    row_num2 = to_items(back2)
    total_num2 = row_num2 + other_core(row_num2)
    return (1.0 - alpha_mix) * prior + alpha_mix * total_num2 / scale


def solution(mesh):
    return jax.shard_map(
        body,
        mesh=mesh,
        in_specs=(P("gx", None), P("gx", None), P("ta", "gx", None)),
        out_specs=P("gx", None),
        check_vma=False,
    )
```

```python
import functools

import jax
import jax.numpy as jnp
from jax import lax
from jax.experimental import pallas as pl
from jax.experimental.pallas import tpu as pltpu
from jax.sharding import PartitionSpec as P

CAP = 2048
PAD_MARK = -1024.0


sharpness = 8.0
alpha_mix = 0.8


def normalize(embeds):
    wide = embeds.astype(jnp.float32)
    return (wide * lax.rsqrt(jnp.sum(wide * wide, axis=1, keepdims=True) + 1e-06)).astype(
        jnp.bfloat16
    )


def a2a_kernel(count, *refs):
    x_refs = refs[:count]
    o_refs = refs[count : 2 * count]
    send_sem, recv_sem, local_sem = refs[2 * count :]
    n = x_refs[0].shape[0]
    me = lax.axis_index("gx")
    core = lax.axis_index("ta")
    mesh_ids = pl.DeviceIdType.MESH
    barrier = pltpu.get_barrier_semaphore()

    def greet(i, carry):
        peer = lax.rem(me + 1 + i, n)
        pl.semaphore_signal(barrier, 1, device_id=(peer, core), device_id_type=mesh_ids)
        return carry

    lax.fori_loop(0, n - 1, greet, 0)
    pl.semaphore_wait(barrier, n - 1)
    locals_ = [
        pltpu.make_async_copy(x.at[me], o.at[me], local_sem.at[k])
        for k, (x, o) in enumerate(zip(x_refs, o_refs))
    ]
    for local in locals_:
        local.start()

    def copy_with(k, peer, block_from, block_to):
        return pltpu.make_async_remote_copy(
            x_refs[k].at[block_from],
            o_refs[k].at[block_to],
            send_sem.at[k, block_from],
            recv_sem.at[k, block_to],
            device_id=(peer, core),
            device_id_type=mesh_ids,
        )

    def partner(i):
        j = n - 2 - i
        return lax.rem(me + (1 - 2 * lax.rem(j, 2)) * (j // 2 + 1) + n, n)

    def send(i, carry):
        peer = partner(i)
        for k in range(count):
            copy_with(k, peer, peer, me).start()
        return carry

    lax.fori_loop(0, n - 1, send, 0)

    def finish(i, carry):
        peer = partner(i)
        for k in range(count):
            copy_with(k, peer, peer, me).wait_send()
            copy_with(k, peer, peer, peer).wait_recv()
        return carry

    lax.fori_loop(0, n - 1, finish, 0)
    for local in locals_:
        local.wait()


def all_to_all(arrays, collective_id):
    count = len(arrays)
    n = arrays[0].shape[0]
    return pl.pallas_call(
        functools.partial(a2a_kernel, count),
        out_shape=[jax.ShapeDtypeStruct(x.shape, x.dtype) for x in arrays],
        in_specs=[pl.BlockSpec(memory_space=pl.ANY)] * count,
        out_specs=[pl.BlockSpec(memory_space=pl.ANY)] * count,
        scratch_shapes=[
            pltpu.SemaphoreType.DMA((count, n)),
            pltpu.SemaphoreType.DMA((count, n)),
            pltpu.SemaphoreType.DMA((count,)),
        ],
        compiler_params=pltpu.CompilerParams(collective_id=collective_id, has_side_effects=True),
    )(*arrays)


def bucket_weights(unit, valid):
    cap = unit.shape[0]
    block = cap
    cols = jnp.arange(cap)
    blocks = []
    dens = []
    for start in range(0, cap, block):
        gram = lax.dot_general(
            unit[start : start + block],
            unit,
            (((1,), (1,)), ((), ())),
            preferred_element_type=jnp.float32,
        )
        keep = valid[None, :] * (cols[None, :] != (start + jnp.arange(block))[:, None]).astype(
            jnp.float32
        )
        weights = (jnp.exp(sharpness * gram) * keep).astype(jnp.bfloat16)
        blocks.append(weights)
        dens.append(jnp.sum(weights.astype(jnp.float32), axis=1))
    return blocks, jnp.concatenate(dens, axis=0)


def weighted_sums(blocks, feats):
    return jnp.concatenate(
        [jnp.dot(w, feats, preferred_element_type=jnp.float32) for w in blocks], axis=0
    )


def body(embeddings, labels, bucket_ids):
    groups = lax.axis_size("gx")
    rows = embeddings.shape[0]
    slot = CAP // groups
    width_l = labels.shape[1]
    ids = bucket_ids[0, :, 0]
    pos = jnp.arange(rows, dtype=jnp.int32)
    same = (ids[:, None] == ids[None, :]) & (pos[None, :] < pos[:, None])
    rank = jnp.sum(same.astype(jnp.int32), axis=1)
    target = ids * slot + rank
    slots = jnp.arange(groups * slot, dtype=jnp.int32)
    place_mat = (target[None, :] == slots[:, None]).astype(jnp.bfloat16)
    occupied = jnp.sum(place_mat.astype(jnp.float32), axis=1) > 0.5
    prior = labels.astype(jnp.float32)

    def place(payload):
        return jnp.dot(place_mat, payload, preferred_element_type=jnp.float32).astype(payload.dtype)

    def to_items(values):
        hi = lax.reduce_precision(values, exponent_bits=8, mantissa_bits=7)
        lo = values - hi
        pick = lambda part: lax.dot_general(
            place_mat,
            part.astype(jnp.bfloat16),
            (((0,), (0,)), ((), ())),
            preferred_element_type=jnp.float32,
        )
        return pick(hi) + pick(lo)

    def exchange(buffer):
        return lax.all_to_all(buffer, "gx", split_axis=0, concat_axis=0, tiled=True)

    def other_core(values):
        return lax.ppermute(values, "ta", perm=[(0, 1), (1, 0)])

    unit_here = normalize(embeddings)
    placed = place(jnp.concatenate([unit_here, labels], axis=1))
    column = lax.broadcasted_iota(jnp.int32, placed.shape, 1)
    pad_here = (column == unit_here.shape[1]) & ~occupied[:, None]
    placed = jnp.where(pad_here, jnp.bfloat16(PAD_MARK), placed)
    got = exchange(placed.reshape(groups, slot, -1)).reshape(groups * slot, -1)
    unit = got[:, : unit_here.shape[1]]
    feats0 = got[:, unit_here.shape[1] :]
    valid = (feats0[:, 0].astype(jnp.float32) > PAD_MARK * 0.5).astype(jnp.float32)

    blocks, den = bucket_weights(unit, valid)
    num1 = weighted_sums(blocks, feats0)

    back_num, back_den = all_to_all([num1.reshape(groups, slot, width_l), den.reshape(groups, slot)], 0)
    back_num = back_num.reshape(groups * slot, width_l)
    back_den = back_den.reshape(groups * slot)
    row_num = to_items(back_num)
    row_den = jnp.sum(jnp.where(target[None, :] == slots[:, None], back_den[:, None], 0.0), axis=0)
    other_num, other_den = other_core((row_num, row_den))
    total_num = row_num + other_num
    total_den = row_den + other_den
    scale = (1.0 + total_den)[:, None]
    first = (1.0 - alpha_mix) * prior + alpha_mix * total_num / scale

    feats1 = exchange(place(first.astype(jnp.bfloat16)).reshape(groups, slot, -1))
    num2 = weighted_sums(blocks, feats1.reshape(groups * slot, -1))
    back2 = exchange(num2.reshape(groups, slot, -1)).reshape(groups * slot, -1)
    row_num2 = to_items(back2)
    total_num2 = row_num2 + other_core(row_num2)
    return (1.0 - alpha_mix) * prior + alpha_mix * total_num2 / scale


def solution(mesh):
    return jax.shard_map(
        body,
        mesh=mesh,
        in_specs=(P("gx", None), P("gx", None), P("ta", "gx", None)),
        out_specs=P("gx", None),
        check_vma=False,
    )
```

```python
import functools

import jax
import jax.numpy as jnp
from jax import lax
from jax.experimental import pallas as pl
from jax.experimental.pallas import tpu as pltpu
from jax.sharding import PartitionSpec as P

CAP = 2048
PAD_MARK = -1024.0


sharpness = 8.0
alpha_mix = 0.8


def normalize(embeds):
    wide = embeds.astype(jnp.float32)
    return (wide * lax.rsqrt(jnp.sum(wide * wide, axis=1, keepdims=True) + 1e-06)).astype(
        jnp.bfloat16
    )


def a2a_kernel(count, *refs):
    x_refs = refs[:count]
    o_refs = refs[count : 2 * count]
    send_sem, recv_sem, local_sem = refs[2 * count :]
    n = x_refs[0].shape[0]
    me = lax.axis_index("gx")
    core = lax.axis_index("ta")
    mesh_ids = pl.DeviceIdType.MESH
    barrier = pltpu.get_barrier_semaphore()

    def greet(i, carry):
        peer = lax.rem(me + 1 + i, n)
        pl.semaphore_signal(barrier, 1, device_id=(peer, core), device_id_type=mesh_ids)
        return carry

    lax.fori_loop(0, n - 1, greet, 0)
    pl.semaphore_wait(barrier, n - 1)
    locals_ = [
        pltpu.make_async_copy(x.at[me], o.at[me], local_sem.at[k])
        for k, (x, o) in enumerate(zip(x_refs, o_refs))
    ]
    for local in locals_:
        local.start()

    def copy_with(k, peer, block_from, block_to):
        return pltpu.make_async_remote_copy(
            x_refs[k].at[block_from],
            o_refs[k].at[block_to],
            send_sem.at[k, block_from],
            recv_sem.at[k, block_to],
            device_id=(peer, core),
            device_id_type=mesh_ids,
        )

    def partner(i):
        j = n - 2 - i
        return lax.rem(me + (1 - 2 * lax.rem(j, 2)) * (j // 2 + 1) + n, n)

    def send(i, carry):
        peer = partner(i)
        for k in range(count):
            copy_with(k, peer, peer, me).start()
        return carry

    lax.fori_loop(0, n - 1, send, 0)

    def finish(i, carry):
        peer = partner(i)
        for k in range(count):
            copy_with(k, peer, peer, me).wait_send()
            copy_with(k, peer, peer, peer).wait_recv()
        return carry

    lax.fori_loop(0, n - 1, finish, 0)
    for local in locals_:
        local.wait()


def all_to_all(arrays, collective_id):
    count = len(arrays)
    n = arrays[0].shape[0]
    return pl.pallas_call(
        functools.partial(a2a_kernel, count),
        out_shape=[jax.ShapeDtypeStruct(x.shape, x.dtype) for x in arrays],
        in_specs=[pl.BlockSpec(memory_space=pl.ANY)] * count,
        out_specs=[pl.BlockSpec(memory_space=pl.ANY)] * count,
        scratch_shapes=[
            pltpu.SemaphoreType.DMA((count, n)),
            pltpu.SemaphoreType.DMA((count, n)),
            pltpu.SemaphoreType.DMA((count,)),
        ],
        compiler_params=pltpu.CompilerParams(collective_id=collective_id, has_side_effects=True),
    )(*arrays)


def bucket_weights(unit, valid):
    cap = unit.shape[0]
    block = cap
    cols = jnp.arange(cap)
    blocks = []
    dens = []
    for start in range(0, cap, block):
        gram = lax.dot_general(
            unit[start : start + block],
            unit,
            (((1,), (1,)), ((), ())),
            preferred_element_type=jnp.float32,
        )
        keep = valid[None, :] * (cols[None, :] != (start + jnp.arange(block))[:, None]).astype(
            jnp.float32
        )
        weights = (jnp.exp(sharpness * gram) * keep).astype(jnp.bfloat16)
        blocks.append(weights)
        dens.append(jnp.sum(weights.astype(jnp.float32), axis=1))
    return blocks, jnp.concatenate(dens, axis=0)


def weighted_sums(blocks, feats):
    return jnp.concatenate(
        [jnp.dot(w, feats, preferred_element_type=jnp.float32) for w in blocks], axis=0
    )


def body(embeddings, labels, bucket_ids):
    groups = lax.axis_size("gx")
    rows = embeddings.shape[0]
    slot = CAP // groups
    width_l = labels.shape[1]
    ids = bucket_ids[0, :, 0]
    pos = jnp.arange(rows, dtype=jnp.int32)
    same = (ids[:, None] == ids[None, :]) & (pos[None, :] < pos[:, None])
    rank = jnp.sum(same.astype(jnp.int32), axis=1)
    target = ids * slot + rank
    slots = jnp.arange(groups * slot, dtype=jnp.int32)
    place_mat = (target[None, :] == slots[:, None]).astype(jnp.bfloat16)
    occupied = jnp.sum(place_mat.astype(jnp.float32), axis=1) > 0.5
    prior = labels.astype(jnp.float32)

    def place(payload):
        return jnp.dot(place_mat, payload, preferred_element_type=jnp.float32).astype(payload.dtype)

    def to_items(values):
        hi = lax.reduce_precision(values, exponent_bits=8, mantissa_bits=7)
        lo = values - hi
        pick = lambda part: lax.dot_general(
            place_mat,
            part.astype(jnp.bfloat16),
            (((0,), (0,)), ((), ())),
            preferred_element_type=jnp.float32,
        )
        return pick(hi) + pick(lo)

    def exchange(buffer):
        return lax.all_to_all(buffer, "gx", split_axis=0, concat_axis=0, tiled=True)

    def other_core(values):
        return lax.ppermute(values, "ta", perm=[(0, 1), (1, 0)])

    def both_tables(values):
        half = values.shape[1] // 2
        parts = []
        for c in range(2):
            mine = to_items(values[:, c * half : (c + 1) * half])
            parts.append(mine + other_core(mine))
        return jnp.concatenate(parts, axis=1)

    unit_here = normalize(embeddings)
    placed = place(jnp.concatenate([unit_here, labels], axis=1))
    column = lax.broadcasted_iota(jnp.int32, placed.shape, 1)
    pad_here = (column == unit_here.shape[1]) & ~occupied[:, None]
    placed = jnp.where(pad_here, jnp.bfloat16(PAD_MARK), placed)
    got = exchange(placed.reshape(groups, slot, -1)).reshape(groups * slot, -1)
    unit = got[:, : unit_here.shape[1]]
    feats0 = got[:, unit_here.shape[1] :]
    valid = (feats0[:, 0].astype(jnp.float32) > PAD_MARK * 0.5).astype(jnp.float32)

    blocks, den = bucket_weights(unit, valid)
    num1 = weighted_sums(blocks, feats0)

    back_num, back_den = all_to_all([num1.reshape(groups, slot, width_l), den.reshape(groups, slot)], 0)
    back_num = back_num.reshape(groups * slot, width_l)
    back_den = back_den.reshape(groups * slot)
    row_den = jnp.sum(jnp.where(target[None, :] == slots[:, None], back_den[:, None], 0.0), axis=0)
    total_den = row_den + other_core(row_den)
    total_num = both_tables(back_num)
    scale = (1.0 + total_den)[:, None]
    first = (1.0 - alpha_mix) * prior + alpha_mix * total_num / scale

    feats1 = exchange(place(first.astype(jnp.bfloat16)).reshape(groups, slot, -1))
    num2 = weighted_sums(blocks, feats1.reshape(groups * slot, -1))
    back2 = exchange(num2.reshape(groups, slot, -1)).reshape(groups * slot, -1)
    total_num2 = both_tables(back2)
    return (1.0 - alpha_mix) * prior + alpha_mix * total_num2 / scale


def solution(mesh):
    return jax.shard_map(
        body,
        mesh=mesh,
        in_specs=(P("gx", None), P("gx", None), P("ta", "gx", None)),
        out_specs=P("gx", None),
        check_vma=False,
    )
```

```python
import functools

import jax
import jax.numpy as jnp
from jax import lax
from jax.experimental import pallas as pl
from jax.experimental.pallas import tpu as pltpu
from jax.sharding import PartitionSpec as P

CAP = 2048
PAD_MARK = -1024.0


sharpness = 8.0
alpha_mix = 0.8


def normalize(embeds):
    wide = embeds.astype(jnp.float32)
    return (wide * lax.rsqrt(jnp.sum(wide * wide, axis=1, keepdims=True) + 1e-06)).astype(
        jnp.bfloat16
    )


def a2a_kernel(count, *refs):
    x_refs = refs[:count]
    o_refs = refs[count : 2 * count]
    send_sem, recv_sem, local_sem = refs[2 * count :]
    n = x_refs[0].shape[0]
    me = lax.axis_index("gx")
    core = lax.axis_index("ta")
    mesh_ids = pl.DeviceIdType.MESH
    barrier = pltpu.get_barrier_semaphore()

    def partner(i):
        j = n - 2 - i
        return lax.rem(me + (1 - 2 * lax.rem(j, 2)) * (j // 2 + 1) + n, n)

    def greet(i, carry):
        pl.semaphore_signal(barrier, 1, device_id=(partner(i), core), device_id_type=mesh_ids)
        return carry

    lax.fori_loop(0, n - 1, greet, 0)
    pl.semaphore_wait(barrier, n - 1)
    locals_ = [
        pltpu.make_async_copy(x.at[me], o.at[me], local_sem.at[k])
        for k, (x, o) in enumerate(zip(x_refs, o_refs))
    ]
    for local in locals_:
        local.start()

    def copy_with(k, peer, block_from, block_to):
        return pltpu.make_async_remote_copy(
            x_refs[k].at[block_from],
            o_refs[k].at[block_to],
            send_sem.at[k, block_from],
            recv_sem.at[k, block_to],
            device_id=(peer, core),
            device_id_type=mesh_ids,
        )

    def send(i, carry):
        peer = partner(i)
        for k in range(count):
            copy_with(k, peer, peer, me).start()
        return carry

    lax.fori_loop(0, n - 1, send, 0)

    def finish(i, carry):
        peer = partner(i)
        for k in range(count):
            copy_with(k, peer, peer, me).wait_send()
            copy_with(k, peer, peer, peer).wait_recv()
        return carry

    lax.fori_loop(0, n - 1, finish, 0)
    for local in locals_:
        local.wait()


def all_to_all(arrays, collective_id):
    count = len(arrays)
    n = arrays[0].shape[0]
    return pl.pallas_call(
        functools.partial(a2a_kernel, count),
        out_shape=[jax.ShapeDtypeStruct(x.shape, x.dtype) for x in arrays],
        in_specs=[pl.BlockSpec(memory_space=pl.ANY)] * count,
        out_specs=[pl.BlockSpec(memory_space=pl.ANY)] * count,
        scratch_shapes=[
            pltpu.SemaphoreType.DMA((count, n)),
            pltpu.SemaphoreType.DMA((count, n)),
            pltpu.SemaphoreType.DMA((count,)),
        ],
        compiler_params=pltpu.CompilerParams(collective_id=collective_id, has_side_effects=True),
    )(*arrays)


def bucket_weights(unit, valid):
    cap = unit.shape[0]
    block = cap
    cols = jnp.arange(cap)
    blocks = []
    dens = []
    for start in range(0, cap, block):
        gram = lax.dot_general(
            unit[start : start + block],
            unit,
            (((1,), (1,)), ((), ())),
            preferred_element_type=jnp.float32,
        )
        keep = valid[None, :] * (cols[None, :] != (start + jnp.arange(block))[:, None]).astype(
            jnp.float32
        )
        weights = (jnp.exp(sharpness * gram) * keep).astype(jnp.bfloat16)
        blocks.append(weights)
        dens.append(jnp.sum(weights.astype(jnp.float32), axis=1))
    return blocks, jnp.concatenate(dens, axis=0)


def weighted_sums(blocks, feats):
    return jnp.concatenate(
        [jnp.dot(w, feats, preferred_element_type=jnp.float32) for w in blocks], axis=0
    )


def body(embeddings, labels, bucket_ids):
    groups = lax.axis_size("gx")
    rows = embeddings.shape[0]
    slot = CAP // groups
    width_l = labels.shape[1]
    ids = bucket_ids[0, :, 0]
    pos = jnp.arange(rows, dtype=jnp.int32)
    same = (ids[:, None] == ids[None, :]) & (pos[None, :] < pos[:, None])
    rank = jnp.sum(same.astype(jnp.int32), axis=1)
    target = ids * slot + rank
    slots = jnp.arange(groups * slot, dtype=jnp.int32)
    place_mat = (target[None, :] == slots[:, None]).astype(jnp.bfloat16)
    occupied = jnp.sum(place_mat.astype(jnp.float32), axis=1) > 0.5
    prior = labels.astype(jnp.float32)

    def place(payload):
        return jnp.dot(place_mat, payload, preferred_element_type=jnp.float32).astype(payload.dtype)

    def to_items(values):
        hi = lax.reduce_precision(values, exponent_bits=8, mantissa_bits=7)
        lo = values - hi
        pick = lambda part: lax.dot_general(
            place_mat,
            part.astype(jnp.bfloat16),
            (((0,), (0,)), ((), ())),
            preferred_element_type=jnp.float32,
        )
        return pick(hi) + pick(lo)

    def exchange(buffer):
        return lax.all_to_all(buffer, "gx", split_axis=0, concat_axis=0, tiled=True)

    def other_core(values):
        return lax.ppermute(values, "ta", perm=[(0, 1), (1, 0)])

    unit_here = normalize(embeddings)
    placed = place(jnp.concatenate([unit_here, labels], axis=1))
    column = lax.broadcasted_iota(jnp.int32, placed.shape, 1)
    pad_here = (column == unit_here.shape[1]) & ~occupied[:, None]
    placed = jnp.where(pad_here, jnp.bfloat16(PAD_MARK), placed)
    got = exchange(placed.reshape(groups, slot, -1)).reshape(groups * slot, -1)
    unit = got[:, : unit_here.shape[1]]
    feats0 = got[:, unit_here.shape[1] :]
    valid = (feats0[:, 0].astype(jnp.float32) > PAD_MARK * 0.5).astype(jnp.float32)

    blocks, den = bucket_weights(unit, valid)
    num1 = weighted_sums(blocks, feats0)

    back_num, back_den = all_to_all([num1.reshape(groups, slot, width_l), den.reshape(groups, slot)], 0)
    back_num = back_num.reshape(groups * slot, width_l)
    back_den = back_den.reshape(groups * slot)
    row_num = to_items(back_num)
    row_den = jnp.sum(jnp.where(target[None, :] == slots[:, None], back_den[:, None], 0.0), axis=0)
    other_num, other_den = other_core((row_num, row_den))
    total_num = row_num + other_num
    total_den = row_den + other_den
    scale = (1.0 + total_den)[:, None]
    first = (1.0 - alpha_mix) * prior + alpha_mix * total_num / scale

    feats1 = exchange(place(first.astype(jnp.bfloat16)).reshape(groups, slot, -1))
    num2 = weighted_sums(blocks, feats1.reshape(groups * slot, -1))
    back2 = exchange(num2.reshape(groups, slot, -1)).reshape(groups * slot, -1)
    row_num2 = to_items(back2)
    total_num2 = row_num2 + other_core(row_num2)
    return (1.0 - alpha_mix) * prior + alpha_mix * total_num2 / scale


def solution(mesh):
    return jax.shard_map(
        body,
        mesh=mesh,
        in_specs=(P("gx", None), P("gx", None), P("ta", "gx", None)),
        out_specs=P("gx", None),
        check_vma=False,
    )
```
